512 devices in a mesh: img: 16 (over y, z_hi, core), ref: 32 (over z_lo, x).
Axes of the slice: x: 4, y: 4, z: 16 (z_hi: 2, z_lo: 8; z = z_hi * 8 + z_lo), core: 2. Of those that a mesh axis runs over, the one named last changes fastest.
Arguments:
- images: float32 [2, 256, 32768], P(None, 'img', 'ref'), may hold values from -6 to 6
- references: float32 [2, 256, 32768], P(None, 'ref', 'img'), may hold values from -2 to 2
- precision: float32 [256], P('img'), may hold values from 0.00390625 to 0.0390625
- shifts: int32 [12, 2], replicated, may hold values from -6 to 6, as said below
- labels: int32 [256], P('ref'), may hold values from 0 to 3
- log_prior: float32 [4], replicated, may hold values from -4 to 4
Outputs:
- new_refs: float32 [2, 256, 32768], P(None, 'ref', 'img')
- class_post: float32 [256, 4], P('img')
The draws below stay inside these ranges and needn't reach their ends.
Inputs may be any that keep to these rules, and one draw needn't show every extreme that they name: `shifts`: both ends of the range occur in every draw.
All inputs are finite; a program needn't handle non-finite values.
Results may differ from the reference program's by a relative error of at most 0.0056.
Values may be sent and summed in bfloat16 or wider, within the bound.
No kernel may reach another device: no remote copies, remote signals or barrier semaphores. Data moves between devices by JAX's collectives and lax.ppermute only.
A program may use at most 64 MiB of HBM per device.

```python
import math
import jax
import jax.numpy as jnp
from jax import lax

ROWS = 256
COLS = 128
SHIFTS = 12
CLASSES = 4
IMAGES = 256
REFS = 256


def shift_table(key):
    base = jax.random.fold_in(key, 202)
    first, second, third = jax.random.split(base, 3)
    table = jax.random.randint(first, (SHIFTS, 2), -6, 7, dtype=jnp.int32)
    low_row = jax.random.randint(second, (), 0, SHIFTS, dtype=jnp.int32)
    high_row = jax.random.randint(third, (), 0, SHIFTS, dtype=jnp.int32)
    row_index = jnp.arange(SHIFTS, dtype=jnp.int32)[:, None]
    col_index = jnp.arange(2, dtype=jnp.int32)[None, :]
    table = jnp.where((row_index == low_row) & (col_index == 0), jnp.int32(-6), table)
    table = jnp.where((row_index == high_row) & (col_index == 1), jnp.int32(6), table)
    return table.astype(jnp.int32)


def ref_table(key):
    base = jax.random.fold_in(key, 101)
    first, second = jax.random.split(base, 2)
    phase = jax.random.uniform(first, (REFS, ROWS * COLS), jnp.float32, -math.pi, math.pi)
    level = jax.random.uniform(second, (REFS, ROWS * COLS), jnp.float32, 0.85, 1.05)
    profile = jnp.ones((1, ROWS * COLS), jnp.float32)
    amplitude = jnp.sqrt(2.0 * profile) * level
    return jnp.stack([amplitude * jnp.cos(phase), amplitude * jnp.sin(phase)]).astype(jnp.float32)


def bright_plan(key):
    base = jax.random.fold_in(key, 404)
    first, second, third, fourth = jax.random.split(base, 4)
    marks = jax.random.randint(first, (IMAGES,), 0, 8, dtype=jnp.int32)
    forced = jax.random.randint(second, (), 0, IMAGES, dtype=jnp.int32)
    bright = (marks == 0) | (jnp.arange(IMAGES, dtype=jnp.int32) == forced)
    strength = jax.random.uniform(third, (IMAGES,), jnp.float32, 150.0, 300.0)
    offset = jax.random.randint(fourth, (IMAGES,), 1, REFS, dtype=jnp.int32)
    return (bright, strength, offset)


def draw_shifts(key, part):
    return shift_table(key)


def draw_references(key, part):
    return ref_table(key)


def draw_precision(key, part):
    bright, strength, offset = bright_plan(key)
    base = jax.random.fold_in(key, 505)
    lo = 1.0 / (2.0 * ROWS * COLS) ** 0.5
    hi = 10.0 / (2.0 * ROWS * COLS) ** 0.5
    drawn = jnp.exp(jax.random.uniform(base, (IMAGES,), jnp.float32, math.log(lo), math.log(hi)))
    return jnp.where(bright, strength / (ROWS * COLS), drawn).astype(jnp.float32)


def draw_images(key, part):
    refs = ref_table(key)
    table = shift_table(key)
    bright, strength, offset = bright_plan(key)
    base = jax.random.fold_in(key, 303)
    first, second, third, fourth, fifth = jax.random.split(base, 5)
    chosen = jax.random.randint(first, (IMAGES,), 0, REFS, dtype=jnp.int32)
    partner = (chosen + offset) % REFS
    which = jax.random.randint(second, (IMAGES,), 0, SHIFTS, dtype=jnp.int32)
    index = jnp.arange(ROWS * COLS, dtype=jnp.int32)
    freq_y = (index // COLS - ROWS // 2).astype(jnp.float32)
    freq_x = (index % COLS).astype(jnp.float32)
    shift_x = table[which, 0].astype(jnp.float32)[:, None]
    shift_y = table[which, 1].astype(jnp.float32)[:, None]
    angles = 2.0 * math.pi / ROWS * (freq_x[None, :] * shift_x + freq_y[None, :] * shift_y)
    cosine = jnp.cos(angles)
    sine_part = jnp.sin(angles)
    picked = refs[:, chosen, :]
    other = refs[:, partner, :]
    signal = jnp.stack([picked[0] * cosine + picked[1] * sine_part, picked[1] * cosine - picked[0] * sine_part])
    second_signal = jnp.stack([other[0] * cosine + other[1] * sine_part, other[1] * cosine - other[0] * sine_part])
    signal_weight = jnp.exp(jax.random.uniform(fourth, (IMAGES,), jnp.float32, 0.0, math.log(48.0)))
    signal_weight = signal_weight / (2.0 * ROWS * COLS) ** 0.5
    noise_level = jax.random.uniform(fifth, (IMAGES,), jnp.float32, 0.75, 1.2)
    noise = jax.random.truncated_normal(third, -4.5, 4.5, (2, IMAGES, ROWS * COLS), jnp.float32)
    drawn = signal_weight[None, :, None] * signal + noise_level[None, :, None] * noise
    mixed = signal + (1.0 - 1.0 / strength)[None, :, None] * second_signal + 0.02 * noise
    result = jnp.where(bright[None, :, None], mixed, drawn)
    return jnp.clip(result, -6.0, 6.0).astype(jnp.float32)


def place_ends(entries, key, least, top_value):
    place = [jax.random.randint(jax.random.fold_in(key, axis), (), 0, length) for axis, length in enumerate(entries.shape)]
    widest = entries.shape.index(max(entries.shape))
    neighbour = place[:widest] + [(place[widest] + 1) % entries.shape[widest]] + place[widest + 1:]
    return entries.at[tuple(place)].set(least).at[tuple(neighbour)].set(top_value)


def normal_values(stream_key, shape, width, most, held_as=jnp.bfloat16):
    return jnp.clip(width * jax.random.normal(stream_key, shape, jnp.float32), -most, most).astype(held_as)


def setup_inputs(seed: int = 0) -> dict:
    keys = jax.random.split(jax.random.key(seed), 7)
    images = draw_images(jax.random.fold_in(keys[6], 71), 0)
    references = draw_references(jax.random.fold_in(keys[6], 71), 0)
    precision = draw_precision(jax.random.fold_in(keys[6], 71), 0)
    shifts = draw_shifts(jax.random.fold_in(keys[6], 71), 0)
    labels = place_ends(jax.random.randint(keys[4], (REFS,), 0, CLASSES), jax.random.fold_in(keys[4], 1), 0, CLASSES - 1).astype(jnp.int32)
    log_prior = normal_values(keys[5], (CLASSES,), 1.0, 4.0, jnp.float32)
    return {"images": images, "references": references, "precision": precision, "shifts": shifts, "labels": labels, "log_prior": log_prior}


def phases(shifts):
    index = jnp.arange(ROWS * COLS, dtype=jnp.int32)
    freq_y = (index // COLS - ROWS // 2).astype(jnp.float32)
    freq_x = (index % COLS).astype(jnp.float32)
    shift_x = shifts[:, 0].astype(jnp.float32)[:, None]
    shift_y = shifts[:, 1].astype(jnp.float32)[:, None]
    angles = (2.0 * math.pi / ROWS) * (freq_x[None, :] * shift_x + freq_y[None, :] * shift_y)
    return jnp.cos(angles), jnp.sin(angles)


def reference(images, references, precision, shifts, labels, log_prior):
    img_low = images.astype(jnp.bfloat16)
    ref_low = references.astype(jnp.bfloat16)
    cosine, sine_part = phases(shifts)
    ref_wide = ref_low.astype(jnp.float32)
    energy = jnp.sum(ref_wide * ref_wide, axis=(0, 2))
    onehot = (labels[:, None] == jnp.arange(CLASSES, dtype=jnp.int32)[None, :]).astype(jnp.float32)
    prior_term = jnp.sum(onehot * log_prior[None, :], axis=1)

    def cross_one(operands):
        cos_row, sin_row = operands
        shifted_re = (ref_wide[0] * cos_row[None, :] + ref_wide[1] * sin_row[None, :]).astype(jnp.bfloat16)
        shifted_im = (ref_wide[1] * cos_row[None, :] - ref_wide[0] * sin_row[None, :]).astype(jnp.bfloat16)
        return (jnp.dot(img_low[0], shifted_re.T, preferred_element_type=jnp.float32)
                + jnp.dot(img_low[1], shifted_im.T, preferred_element_type=jnp.float32))

    cross_terms = lax.map(cross_one, (cosine, sine_part))
    scores = precision[None, :, None] * (cross_terms - 0.5 * energy[None, None, :]) + prior_term[None, None, :]
    top_score = jnp.max(scores, axis=(0, 2))
    exponent = jnp.exp(scores - top_score[None, :, None])
    row_total = jnp.sum(exponent, axis=(0, 2))
    posterior = exponent / row_total[None, :, None]
    class_post = jnp.einsum("ik,kc->ic", jnp.sum(posterior, axis=0), onehot, precision=lax.Precision.HIGHEST)
    ref_mass = jnp.sum(posterior, axis=(0, 1))
    post_low = posterior.astype(jnp.bfloat16)

    def back_one(running, operands):
        weights_row, cos_row, sin_row = operands
        back_re = jnp.dot(weights_row.T, img_low[0], preferred_element_type=jnp.float32)
        back_im = jnp.dot(weights_row.T, img_low[1], preferred_element_type=jnp.float32)
        update = jnp.stack([back_re * cos_row[None, :] - back_im * sin_row[None, :],
                            back_im * cos_row[None, :] + back_re * sin_row[None, :]])
        return running + update, None

    start_sum = jnp.zeros((2, labels.shape[0], ROWS * COLS), jnp.float32)
    summed, unused = lax.scan(back_one, start_sum, (post_low, cosine, sine_part))
    new_refs = summed / (ref_mass + 1.0)[None, :, None]
    return new_refs, class_post
```

```python
import math

import jax
import jax.numpy as jnp
from jax import lax
from jax.experimental import pallas as pl
from jax.experimental.pallas import tpu as pltpu
from jax.sharding import Mesh
from jax.sharding import PartitionSpec as P

ROWS = 256
COLS = 128
SHIFTS = 12
CLASSES = 4
LANES = 128
USED = SHIFTS * 8
SIZES = {"y": 4, "zh": 2, "c": 2, "zl": 8, "x": 4}
ALL = ("y", "zh", "c", "zl", "x")
SPACE = ("y", "c", "x")
IMG = ("y", "zh", "c")
REF = ("zl", "x")


def place(y, zh, c, zl, x):
    return (((y * 2 + zh) * 2 + c) * 8 + zl) * 4 + x


def every():
    return [
        (y, zh, c, zl, x)
        for y in range(4)
        for zh in range(2)
        for c in range(2)
        for zl in range(8)
        for x in range(4)
    ]


REF_ROUTE = [
    (place(y, zh, c, zl, x), place(zl // 2, zh, zl % 2, y * 2 + c, x)) for y, zh, c, zl, x in every()
]
IMG_ROUTE = [
    (place(y, zh, c, zl, x), place(y, zl & 1, c, (zl >> 1) * 2 + (x >> 1), zh * 2 + (x & 1)))
    for y, zh, c, zl, x in every()
]


def phases(shifts, block):
    index = block * 2048 + jnp.arange(2048, dtype=jnp.int32)
    freq_y = (index // COLS - ROWS // 2).astype(jnp.float32)
    freq_x = (index % COLS).astype(jnp.float32)
    shift_x = shifts[:, 0].astype(jnp.float32)[:, None]
    shift_y = shifts[:, 1].astype(jnp.float32)[:, None]
    angles = 2.0 * math.pi / ROWS * (freq_x[None, :] * shift_x + freq_y[None, :] * shift_y)
    return jnp.cos(angles), jnp.sin(angles)


def own_lanes():
    lane = lax.broadcasted_iota(jnp.int32, (8, LANES), 1)
    row = lax.broadcasted_iota(jnp.int32, (8, LANES), 0)
    return (lane % 8 == row) & (lane < USED)


def cross_kernel(img_ref, ref_ref, cos_ref, sin_ref, label_ref, out_ref, shifted):
    re = ref_ref[0].astype(jnp.float32)
    im = ref_ref[1].astype(jnp.float32)
    energy = jnp.sum(re * re + im * im, axis=1, keepdims=True)
    half = jnp.sum(jnp.where(own_lanes(), 0.5 * energy, 0.0), axis=0, keepdims=True)
    for pair in range(SHIFTS // 2):
        rot_re, rot_im = [], []
        for t in (2 * pair, 2 * pair + 1):
            cos, sin = cos_ref[t : t + 1, :], sin_ref[t : t + 1, :]
            rot_re.append(re * cos + im * sin)
            rot_im.append(im * cos - re * sin)
        rows = slice(16 * pair, 16 * pair + 16)
        shifted[0, rows, :] = jnp.concatenate(rot_re, axis=0).astype(jnp.bfloat16)
        shifted[1, rows, :] = jnp.concatenate(rot_im, axis=0).astype(jnp.bfloat16)
    shifted[:, USED:, :] = jnp.zeros((2, LANES - USED, 2048), jnp.bfloat16)
    total = jnp.zeros((256, LANES), jnp.float32)
    for h in range(2):
        for part in range(2):
            total += lax.dot_general(
                img_ref[:, :, :, h, part].reshape(256, 1024),
                shifted[part, :, h * 1024 : (h + 1) * 1024],
                (((1,), (1,)), ((), ())),
                preferred_element_type=jnp.float32,
            )
    total = (total - half + label_ref[...]).reshape(4, 2, 2, 16, LANES)
    for y in range(4):
        for c in range(2):
            for zh in range(2):
                for copy in range(2):
                    out_ref[(y * 2 + zh) * 2 + c, copy] = total[y, c, zh]


def softmax_kernel(got_ref, prior_ref, precision_ref, out_ref):
    both = got_ref[:, 0] + got_ref[:, 1]
    tile = both[:, :, 0:8] + both[:, :, 8:16] + both[:, :, 16:24] + both[:, :, 24:32]
    row = lax.broadcasted_iota(jnp.int32, (8, LANES), 0)
    lane = lax.broadcasted_iota(jnp.int32, (8, LANES), 1)
    low = row < 4
    scores, labels = [], []
    for y in range(4):
        label = jnp.where(lane < USED, 0.0, got_ref[0, 0, 0, 8 * y : 8 * y + 8, :])
        label = label + pltpu.roll(label, 32, 1)
        label = label + pltpu.roll(label, 64, 1)
        labels.append(label)
        prior = jnp.zeros((8, LANES), jnp.float32)
        for k in range(CLASSES):
            prior = jnp.where(label == k, prior_ref[k], prior)
        first = tile[y, 0] + pltpu.roll(tile[y, 0], 4, 0)
        second = tile[y, 1] + pltpu.roll(tile[y, 1], 4, 0)
        cross = jnp.where(low, first, second)
        score = precision_ref[0] * cross + prior
        scores.append(jnp.where(lane < USED, score, -jnp.inf))
    top = jnp.max(jnp.maximum(jnp.maximum(scores[0], scores[1]), jnp.maximum(scores[2], scores[3])))
    weights = [jnp.exp(score - top) for score in scores]
    total = jnp.sum(weights[0] + weights[1] + weights[2] + weights[3])
    posts = [weight / total for weight in weights]
    classes = jnp.zeros((8, LANES), jnp.float32)
    for k in range(CLASSES):
        mass = sum(jnp.where(labels[y] == k, posts[y], 0.0) for y in range(4))
        classes = jnp.where(lane == USED + k, jnp.sum(mass), classes)
    for y in range(4):
        post = jnp.where(lane < USED, posts[y], classes)
        turned = pltpu.roll(post, 4, 0)
        for c in range(2):
            message = jnp.where(low, post, turned) if c == 0 else jnp.where(low, turned, post)
            for zh in range(2):
                for pair in range(4):
                    out_ref[y, zh, c, 8 * pair : 8 * pair + 8, :] = message


def back_kernel(got_ref, img_ref, cos_ref, sin_ref, out_ref):
    lane = lax.broadcasted_iota(jnp.int32, (256, LANES), 1)
    post = jnp.concatenate(
        [got_ref[(y * 2 + zh) * 2 + c, 0] for y in range(4) for c in range(2) for zh in range(2)], axis=0
    )
    post = jnp.where(lane < USED, post, 0.0)
    mass_row = jnp.sum(post, axis=0, keepdims=True)
    mass = jnp.sum(jnp.where(own_lanes(), mass_row, 0.0), axis=1, keepdims=True)
    weights = jnp.transpose(post).astype(jnp.bfloat16)
    for h in range(2):
        cols = slice(h * 1024, (h + 1) * 1024)
        back = [
            jnp.dot(
                weights,
                img_ref[:, :, :, h, part].reshape(256, 1024),
                preferred_element_type=jnp.float32,
            )
            for part in range(2)
        ]
        sum_re = jnp.zeros((8, 1024), jnp.float32)
        sum_im = jnp.zeros((8, 1024), jnp.float32)
        for t in range(SHIFTS):
            cos, sin = cos_ref[t : t + 1, cols], sin_ref[t : t + 1, cols]
            back_re, back_im = back[0][8 * t : 8 * t + 8], back[1][8 * t : 8 * t + 8]
            sum_re += back_re * cos - back_im * sin
            sum_im += back_im * cos + back_re * sin
        out_ref[0, :, cols] = sum_re / (mass + 1.0)
        out_ref[1, :, cols] = sum_im / (mass + 1.0)


def vmem(count):
    return [pl.BlockSpec(memory_space=pltpu.VMEM)] * count


def call(kernel, shape, dtype, args, scratch=(), specs=None):
    return pl.pallas_call(
        kernel,
        out_shape=jax.ShapeDtypeStruct(shape, dtype),
        in_specs=specs or vmem(len(args)),
        out_specs=pl.BlockSpec(memory_space=pltpu.VMEM),
        scratch_shapes=list(scratch),
        compiler_params=pltpu.CompilerParams(vmem_limit_bytes=32 << 20),
    )(*args)


def local(images, references, precision, shifts, labels, log_prior):
    y, zh, c, zl, x = (lax.axis_index(name) for name in ALL)
    img_low = lax.ppermute(images.astype(jnp.bfloat16), ALL, IMG_ROUTE)
    ref_low = lax.ppermute(references.astype(jnp.bfloat16), ALL, REF_ROUTE)
    label_lanes = jnp.concatenate([jnp.zeros((USED,), jnp.float32), jnp.tile(labels.astype(jnp.float32), 4)])
    units = lax.all_to_all(
        jnp.broadcast_to(img_low[None], (32,) + img_low.shape), SPACE, 0, 0, tiled=True
    )
    units = units.reshape(4, 2, 2, 2, 2, 16, 1024)
    cosine, sine = phases(shifts, (zl // 2) * 4 + zh * 2 + zl % 2)
    cross = call(
        cross_kernel,
        (16, 2, 16, LANES),
        jnp.float32,
        (units, ref_low, cosine, sine, label_lanes[None]),
        [pltpu.VMEM((2, LANES, 2048), jnp.bfloat16)],
    )
    got = lax.all_to_all(cross.reshape(512, 1, LANES), ALL, 0, 0, tiled=True)
    own = lax.dynamic_slice_in_dim(precision, (zl % 4) * 4 + x, 1)
    post = call(
        softmax_kernel,
        (4, 2, 2, 32, LANES),
        jnp.float32,
        (got.reshape(4, 2, 2, 32, LANES), log_prior, own),
        specs=vmem(1) + [pl.BlockSpec(memory_space=pltpu.SMEM)] * 2,
    )
    back = lax.all_to_all(post.reshape(512, 1, LANES), ALL, 0, 0, tiled=True).reshape(16, 2, 16, LANES)
    summed = call(back_kernel, (2, 8, 2048), jnp.float32, (back, units, cosine, sine))
    new_refs = lax.ppermute(summed, ALL, REF_ROUTE)
    mine = lax.dynamic_slice_in_dim(back, (y * 2 + zh) * 2 + c, 1, 0)
    class_post = mine[0, 0, :, USED : USED + CLASSES]
    return new_refs, class_post


def solution(mesh):
    whole = Mesh(mesh.devices.reshape(tuple(SIZES.values())), tuple(SIZES))
    return jax.shard_map(
        local,
        mesh=whole,
        in_specs=(P(None, IMG, REF), P(None, REF, IMG), P(IMG), P(), P(REF), P()),
        out_specs=(P(None, REF, IMG), P(IMG, None)),
        check_vma=False,
    )
```

```python
import itertools
import math

import jax
import jax.numpy as jnp
from jax import lax
from jax.experimental import pallas as pl
from jax.experimental.pallas import tpu as pltpu
from jax.sharding import Mesh
from jax.sharding import PartitionSpec as P

ROWS = 256
COLS = 128
SHIFTS = 12
CLASSES = 4
LANES = 128
USED = SHIFTS * 8
PIXELS = 2048
HALF = 1024
SIZES = {"y": 4, "zh": 2, "c": 2, "zl": 8, "xh": 2, "xl": 2}
ALL = tuple(SIZES)
IMG = ("y", "zh", "c")
REF = ("zl", "xh", "xl")
SPACE = ("y", "c", "xl")
BLOCK = ("zl", "xh")


def place(*coords):
    number = 0
    for size, coord in zip(SIZES.values(), coords, strict=True):
        number = number * size + coord
    return number


def routes(inward):
    made = []
    for r in range(2):
        pairs = []
        for y, zh, c, zl, xh, xl in itertools.product(*(range(size) for size in SIZES.values())):
            work = place(y, zh, c, zl, xh, xl)
            home = place(zl // 2, zl % 2, xh, 2 * y + c, r ^ zh, xl)
            pairs.append((home, work) if inward else (work, home))
        made.append(pairs)
    return made


def phases(shifts, block):
    index = block * PIXELS + jnp.arange(PIXELS, dtype=jnp.int32)
    freq_y = (index // COLS - ROWS // 2).astype(jnp.float32)
    freq_x = (index % COLS).astype(jnp.float32)
    shift_x = shifts[:, 0].astype(jnp.float32)[:, None]
    shift_y = shifts[:, 1].astype(jnp.float32)[:, None]
    angles = 2.0 * math.pi / ROWS * (freq_x[None, :] * shift_x + freq_y[None, :] * shift_y)
    return jnp.cos(angles), jnp.sin(angles)


def iota(shape, axis):
    return lax.broadcasted_iota(jnp.int32, shape, axis)


def own_lanes():
    lane = iota((8, LANES), 1)
    return (lane % 8 == iota((8, LANES), 0)) & (lane < USED)


def as_row(column):
    return jnp.sum(jnp.where(own_lanes(), column, 0.0), axis=0, keepdims=True)


def image_kernel(img_ref, precision_ref, out_ref):
    low = img_ref[...].astype(jnp.bfloat16)
    precision = jnp.sum(
        jnp.where(iota((16, 16), 0) == iota((16, 16), 1), precision_ref[...], 0.0), axis=1, keepdims=True
    )
    first = precision.astype(jnp.bfloat16).astype(jnp.float32)
    second = (precision - first).astype(jnp.bfloat16).astype(jnp.float32)
    third = precision - first - second
    lane = iota((16, LANES), 1)
    pieces = jnp.where(lane == 0, first, jnp.where(lane == 1, second, jnp.where(lane == 2, third, 0.0)))
    pieces = pieces.astype(jnp.bfloat16)
    for copy in range(16):
        out_ref[copy, :, :, :HALF] = low
        out_ref[copy, 0, :, HALF:] = pieces
        out_ref[copy, 1, :, HALF:] = pieces


def ref_kernel(ref_ref, label_ref, out_ref):
    out_ref[:, :, :PIXELS] = ref_ref[...].astype(jnp.bfloat16)
    label = label_ref[...].astype(jnp.float32)
    label = jnp.sum(jnp.where(iota((8, 8), 0) == iota((8, 8), 1), label, 0.0), axis=1, keepdims=True)
    label = jnp.broadcast_to(label, (8, LANES)).astype(jnp.bfloat16)
    out_ref[0, :, PIXELS:] = label
    out_ref[1, :, PIXELS:] = label


def cross_kernel(img_ref, ref0_ref, ref1_ref, cos_ref, sin_ref, zh_ref, out_ref, shifted):
    straight = zh_ref[0] == 0
    ref0 = ref0_ref[:, :, :PIXELS].astype(jnp.float32)
    ref1 = ref1_ref[:, :, :PIXELS].astype(jnp.float32)
    halves = []
    for e in range(2):
        ref = jnp.where(straight, ref0, ref1) if e == 0 else jnp.where(straight, ref1, ref0)
        re, im = ref[0], ref[1]
        halves.append(as_row(0.5 * jnp.sum(re * re + im * im, axis=1, keepdims=True)))
        for pair in range(SHIFTS // 2):
            rot_re, rot_im = [], []
            for t in (2 * pair, 2 * pair + 1):
                cos, sin = cos_ref[t : t + 1, :], sin_ref[t : t + 1, :]
                rot_re.append(re * cos + im * sin)
                rot_im.append(im * cos - re * sin)
            rows = slice(e * LANES + 16 * pair, e * LANES + 16 * pair + 16)
            shifted[0, rows, :] = jnp.concatenate(rot_re, axis=0).astype(jnp.bfloat16)
            shifted[1, rows, :] = jnp.concatenate(rot_im, axis=0).astype(jnp.bfloat16)
        spare = slice(e * LANES + USED, (e + 1) * LANES)
        shifted[:, spare, :] = jnp.zeros((2, LANES - USED, PIXELS), jnp.bfloat16)
    total = jnp.zeros((128, 2 * LANES), jnp.float32)
    for h in range(2):
        for part in range(2):
            total += lax.dot_general(
                img_ref[:, h, part, :, :HALF].reshape(128, HALF),
                shifted[part, :, h * HALF : (h + 1) * HALF],
                (((1,), (1,)), ((), ())),
                preferred_element_type=jnp.float32,
            )
    pieces = img_ref[:, 0, 0, :, HALF:].reshape(128, LANES).astype(jnp.float32)
    precision = jnp.sum(pieces, axis=1, keepdims=True)
    scaled = precision * (total - jnp.concatenate(halves, axis=1))
    out_ref[...] = scaled.reshape(16, 8, 2 * LANES)


def label_rows(ref0_ref, ref1_ref, straight):
    first = ref0_ref[0].astype(jnp.float32)
    second = ref1_ref[0].astype(jnp.float32)
    low, high = jnp.where(straight, first, second), jnp.where(straight, second, first)
    return jnp.concatenate([as_row(low), as_row(high)], axis=1)


def score_kernel(got_ref, ref0_ref, ref1_ref, prior_ref, zh_ref, score_ref, out_ref):
    labels = label_rows(ref0_ref, ref1_ref, zh_ref[0] == 0)
    prior = jnp.zeros((1, 2 * LANES), jnp.float32)
    for k in range(CLASSES):
        prior = jnp.where(labels == k, prior_ref[k], prior)
    scores = jnp.sum(got_ref[...], axis=0) + prior
    scores = jnp.where(iota((8, 2 * LANES), 1) % LANES < USED, scores, -jnp.inf)
    score_ref[...] = scores
    top = jnp.max(scores, axis=1, keepdims=True)
    weights = jnp.exp(scores - top)
    lane = iota((8, LANES), 1)
    stats = jnp.where(lane == 0, top, 0.0)
    for k in range(CLASSES):
        mass = jnp.sum(jnp.where(labels == k, weights, 0.0), axis=1, keepdims=True)
        stats = jnp.where(lane == k + 1, mass, stats)
    out_ref[...] = jnp.broadcast_to(stats[None], (16, 8, LANES))


def post_kernel(got_ref, score_ref, out_ref):
    got = got_ref[...]
    tops = got[:, :, 0:1]
    top = jnp.max(tops, axis=0)
    lane = iota((8, LANES), 1)
    sums = jnp.sum(got * jnp.exp(tops - top[None]), axis=0)
    sums = jnp.where((lane > 0) & (lane <= CLASSES), sums, 0.0)
    total = jnp.sum(sums, axis=1, keepdims=True)
    classes = pltpu.roll(sums / total, USED - 1, 1)
    post = jnp.exp(score_ref[...] - top) / total
    post = jnp.concatenate([jnp.where(lane < USED, post[:, :LANES], classes), post[:, LANES:]], axis=1)
    out_ref[...] = jnp.broadcast_to(post[None], (16, 8, 2 * LANES))


def back_kernel(got_ref, img_ref, cos_ref, sin_ref, zh_ref, out0_ref, out1_ref):
    straight = zh_ref[0] == 0
    post = got_ref[...].reshape(128, 2 * LANES)
    post = jnp.where(iota((128, 2 * LANES), 1) % LANES < USED, post, 0.0)
    mass_row = jnp.sum(post, axis=0, keepdims=True)
    weights = jnp.transpose(post).astype(jnp.bfloat16)
    for h in range(2):
        cols = slice(h * HALF, (h + 1) * HALF)
        back = [
            jnp.dot(
                weights,
                img_ref[:, h, part, :, :HALF].reshape(128, HALF),
                preferred_element_type=jnp.float32,
            )
            for part in range(2)
        ]
        sums = [jnp.zeros((8, HALF), jnp.float32) for both in range(4)]
        for t in range(SHIFTS):
            cos, sin = cos_ref[t : t + 1, cols], sin_ref[t : t + 1, cols]
            for e in range(2):
                rows = slice(e * LANES + 8 * t, e * LANES + 8 * t + 8)
                back_re, back_im = back[0][rows], back[1][rows]
                sums[2 * e] += back_re * cos - back_im * sin
                sums[2 * e + 1] += back_im * cos + back_re * sin
        for part in range(2):
            out0_ref[part, :, cols] = jnp.where(straight, sums[part], sums[2 + part])
            out1_ref[part, :, cols] = jnp.where(straight, sums[2 + part], sums[part])
    masses = []
    for e in range(2):
        row = mass_row[:, e * LANES : (e + 1) * LANES]
        mass = jnp.sum(jnp.where(own_lanes(), row, 0.0), axis=1, keepdims=True)
        masses.append(jnp.broadcast_to(mass, (8, LANES)))
    for part in range(2):
        out0_ref[part, :, PIXELS:] = jnp.where(straight, masses[0], masses[1])
        out1_ref[part, :, PIXELS:] = jnp.where(straight, masses[1], masses[0])


def call(kernel, shapes, args, scratch=(), scalars=0):
    in_vmem = [pl.BlockSpec(memory_space=pltpu.VMEM)] * (len(args) - scalars)
    in_smem = [pl.BlockSpec(memory_space=pltpu.SMEM)] * scalars
    out = [jax.ShapeDtypeStruct(shape, dtype) for shape, dtype in shapes]
    return pl.pallas_call(
        kernel,
        out_shape=out,
        in_specs=in_vmem + in_smem,
        out_specs=[pl.BlockSpec(memory_space=pltpu.VMEM)] * len(out),
        scratch_shapes=list(scratch),
        compiler_params=pltpu.CompilerParams(vmem_limit_bytes=32 << 20),
    )(*args)


def swap(operand, axes):
    return lax.all_to_all(operand, axes, 0, 0, tiled=True)


def local(images, references, precision, shifts, labels, log_prior):
    y, zh, c, zl, xh, xl = (lax.axis_index(name) for name in ALL)
    half = zh.astype(jnp.int32)[None]
    (sent,) = call(image_kernel, [((16, 2, 16, HALF + LANES), jnp.bfloat16)], (images, precision[None]))
    units = swap(sent, SPACE).reshape(8, 2, 2, 16, HALF + LANES)
    (low,) = call(ref_kernel, [((2, 8, PIXELS + LANES), jnp.bfloat16)], (references, labels[None]))
    refs = [lax.ppermute(low, ALL, route) for route in routes(True)]
    tags = [ref[:1, :, PIXELS:] for ref in refs]
    cosine, sine = phases(shifts, zl * 2 + xh)
    (cross,) = call(
        cross_kernel,
        [((16, 8, 2 * LANES), jnp.float32)],
        (units, *refs, cosine, sine, half),
        [pltpu.VMEM((2, 2 * LANES, PIXELS), jnp.bfloat16)],
        scalars=1,
    )
    scores, stats = call(
        score_kernel,
        [((8, 2 * LANES), jnp.float32), ((16, 8, LANES), jnp.float32)],
        (swap(cross, BLOCK), *tags, log_prior, half),
        scalars=2,
    )
    (post,) = call(post_kernel, [((16, 8, 2 * LANES), jnp.float32)], (swap(stats, SPACE), scores))
    posts = swap(post, BLOCK)
    partial = call(
        back_kernel,
        [((2, 8, PIXELS + LANES), jnp.float32)] * 2,
        (posts, units, cosine, sine, half),
        scalars=1,
    )
    first, second = [lax.ppermute(part, ALL, route) for part, route in zip(partial, routes(False), strict=True)]
    both = first + second
    new_refs = both[:, :, :PIXELS] / (both[:, :, PIXELS : PIXELS + 1] + 1.0)
    mine = lax.dynamic_slice_in_dim(posts, (y * 2 + c) * 2, 2, 0)
    class_post = mine.reshape(16, 2 * LANES)[:, USED : USED + CLASSES]
    return new_refs, class_post


def solution(mesh):
    whole = Mesh(mesh.devices.reshape(tuple(SIZES.values())), ALL)
    return jax.shard_map(
        local,
        mesh=whole,
        in_specs=(P(None, IMG, REF), P(None, REF, IMG), P(IMG), P(), P(REF), P()),
        out_specs=(P(None, REF, IMG), P(IMG, None)),
        check_vma=False,
    )
```

```python
import itertools
import math

import jax
import jax.numpy as jnp
from jax import lax
from jax.experimental import pallas as pl
from jax.experimental.pallas import tpu as pltpu
from jax.sharding import Mesh
from jax.sharding import PartitionSpec as P

ROWS = 256
COLS = 128
SHIFTS = 12
CLASSES = 4
LANES = 128
USED = SHIFTS * 8
MASS = USED
CLASS = USED + 4
PIXELS = 2048
HALF = 1024
SIZES = {"y": 4, "zh": 2, "c": 2, "zl": 8, "xh": 2, "xl": 2}
ALL = tuple(SIZES)
IMG = ("y", "zh", "c")
REF = ("zl", "xh", "xl")
SPACE = ("y", "c", "xl")
BLOCK = ("zl", "xh")


def place(*coords):
    number = 0
    for size, coord in zip(SIZES.values(), coords, strict=True):
        number = number * size + coord
    return number


def routes(inward):
    made = []
    for r in range(2):
        pairs = []
        for y, zh, c, zl, xh, xl in itertools.product(*(range(size) for size in SIZES.values())):
            work = place(y, zh, c, zl, xh, xl)
            home = place(zl // 2, zl % 2, xh, 2 * y + c, r ^ zh, xl)
            pairs.append((home, work) if inward else (work, home))
        made.append(pairs)
    return made


def phases(shifts, block):
    index = block * PIXELS + jnp.arange(PIXELS, dtype=jnp.int32)
    freq_y = (index // COLS - ROWS // 2).astype(jnp.float32)
    freq_x = (index % COLS).astype(jnp.float32)
    shift_x = shifts[:, 0].astype(jnp.float32)[:, None]
    shift_y = shifts[:, 1].astype(jnp.float32)[:, None]
    angles = 2.0 * math.pi / ROWS * (freq_x[None, :] * shift_x + freq_y[None, :] * shift_y)
    return jnp.cos(angles), jnp.sin(angles)


def iota(shape, axis):
    return lax.broadcasted_iota(jnp.int32, shape, axis)


def own_lanes():
    lane = iota((8, LANES), 1)
    return (lane % 8 == iota((8, LANES), 0)) & (lane < USED)


def as_row(column):
    return jnp.sum(jnp.where(own_lanes(), column, 0.0), axis=0, keepdims=True)


def pieces_of(value):
    first = value.astype(jnp.bfloat16).astype(jnp.float32)
    second = (value - first).astype(jnp.bfloat16).astype(jnp.float32)
    return first, second, value - first - second


def image_kernel(img_ref, precision_ref, out_ref):
    low = img_ref[...].astype(jnp.bfloat16)
    precision = jnp.sum(
        jnp.where(iota((16, 16), 0) == iota((16, 16), 1), precision_ref[...], 0.0), axis=1, keepdims=True
    )
    first, second, third = pieces_of(precision)
    lane = iota((16, LANES), 1)
    pieces = jnp.where(lane == 0, first, jnp.where(lane == 1, second, jnp.where(lane == 2, third, 0.0)))
    pieces = pieces.astype(jnp.bfloat16)
    for copy in range(16):
        out_ref[copy, :, :, :HALF] = low
        out_ref[copy, 0, :, HALF:] = pieces
        out_ref[copy, 1, :, HALF:] = pieces


def ref_kernel(ref_ref, label_ref, out_ref):
    out_ref[:, :, :PIXELS] = ref_ref[...].astype(jnp.bfloat16)
    label = label_ref[...].astype(jnp.float32)
    label = jnp.sum(jnp.where(iota((8, 8), 0) == iota((8, 8), 1), label, 0.0), axis=1, keepdims=True)
    label = jnp.broadcast_to(label, (8, LANES)).astype(jnp.bfloat16)
    out_ref[0, :, PIXELS:] = label
    out_ref[1, :, PIXELS:] = label


def cross_kernel(img_ref, ref0_ref, ref1_ref, cos_ref, sin_ref, zh_ref, out_ref, shifted):
    straight = zh_ref[0] == 0
    ref0 = ref0_ref[:, :, :PIXELS].astype(jnp.float32)
    ref1 = ref1_ref[:, :, :PIXELS].astype(jnp.float32)
    halves = []
    for e in range(2):
        ref = jnp.where(straight, ref0, ref1) if e == 0 else jnp.where(straight, ref1, ref0)
        re, im = ref[0], ref[1]
        halves.append(as_row(0.5 * jnp.sum(re * re + im * im, axis=1, keepdims=True)))
        for pair in range(SHIFTS // 2):
            rot_re, rot_im = [], []
            for t in (2 * pair, 2 * pair + 1):
                cos, sin = cos_ref[t : t + 1, :], sin_ref[t : t + 1, :]
                rot_re.append(re * cos + im * sin)
                rot_im.append(im * cos - re * sin)
            rows = slice(e * LANES + 16 * pair, e * LANES + 16 * pair + 16)
            shifted[0, rows, :] = jnp.concatenate(rot_re, axis=0).astype(jnp.bfloat16)
            shifted[1, rows, :] = jnp.concatenate(rot_im, axis=0).astype(jnp.bfloat16)
        spare = slice(e * LANES + USED, (e + 1) * LANES)
        shifted[:, spare, :] = jnp.zeros((2, LANES - USED, PIXELS), jnp.bfloat16)
    total = jnp.zeros((128, 2 * LANES), jnp.float32)
    for h in range(2):
        for part in range(2):
            total += lax.dot_general(
                img_ref[:, h, part, :, :HALF].reshape(128, HALF),
                shifted[part, :, h * HALF : (h + 1) * HALF],
                (((1,), (1,)), ((), ())),
                preferred_element_type=jnp.float32,
            )
    pieces = img_ref[:, 0, 0, :, HALF:].reshape(128, LANES).astype(jnp.float32)
    precision = jnp.sum(pieces, axis=1, keepdims=True)
    scaled = precision * (total - jnp.concatenate(halves, axis=1))
    out_ref[...] = scaled.reshape(16, 8, 2 * LANES)


def label_rows(ref0_ref, ref1_ref, straight):
    first = ref0_ref[0].astype(jnp.float32)
    second = ref1_ref[0].astype(jnp.float32)
    low, high = jnp.where(straight, first, second), jnp.where(straight, second, first)
    return jnp.concatenate([as_row(low), as_row(high)], axis=1)


def score_kernel(got_ref, ref0_ref, ref1_ref, prior_ref, zh_ref, score_ref, out_ref):
    labels = label_rows(ref0_ref, ref1_ref, zh_ref[0] == 0)
    prior = jnp.zeros((1, 2 * LANES), jnp.float32)
    for k in range(CLASSES):
        prior = jnp.where(labels == k, prior_ref[k], prior)
    scores = jnp.sum(got_ref[...], axis=0) + prior
    scores = jnp.where(iota((8, 2 * LANES), 1) % LANES < USED, scores, -jnp.inf)
    score_ref[...] = scores
    top = jnp.max(scores, axis=1, keepdims=True)
    weights = jnp.exp(scores - top)
    lane = iota((8, LANES), 1)
    stats = jnp.where(lane == 0, top, 0.0)
    for k in range(CLASSES):
        mass = jnp.sum(jnp.where(labels == k, weights, 0.0), axis=1, keepdims=True)
        stats = jnp.where(lane == k + 1, mass, stats)
    out_ref[...] = jnp.broadcast_to(stats[None], (16, 8, LANES))


def post_kernel(got_ref, score_ref, out_ref):
    got = got_ref[...]
    tops = got[:, :, 0:1]
    top = jnp.max(tops, axis=0)
    lane = iota((8, LANES), 1)
    sums = jnp.sum(got * jnp.exp(tops - top[None]), axis=0)
    sums = jnp.where((lane > 0) & (lane <= CLASSES), sums, 0.0)
    total = jnp.sum(sums, axis=1, keepdims=True)
    classes = pieces_of(sums / total)
    post = jnp.exp(score_ref[...] - top) / total
    mass_row = jnp.sum(post, axis=0, keepdims=True)
    for e in range(2):
        half = slice(e * LANES, (e + 1) * LANES)
        mass = jnp.sum(jnp.where(own_lanes(), mass_row[:, half], 0.0), axis=1, keepdims=True)
        message = jnp.where(lane < USED, post[:, half], 0.0)
        for number, piece in enumerate(pieces_of(mass)):
            message = jnp.where(lane == MASS + number, piece, message)
        if e == 0:
            for number, piece in enumerate(classes):
                message += pltpu.roll(piece, CLASS + CLASSES * number - 1, 1)
        out_ref[:, :, half] = jnp.broadcast_to(message.astype(jnp.bfloat16)[None], (16, 8, LANES))


def back_kernel(got_ref, img_ref, cos_ref, sin_ref, zh_ref, out0_ref, out1_ref):
    straight = zh_ref[0] == 0
    got = got_ref[...].astype(jnp.float32)
    extra = jnp.sum(got, axis=0)
    post = got.reshape(128, 2 * LANES)
    post = jnp.where(iota((128, 2 * LANES), 1) % LANES < USED, post, 0.0)
    weights = jnp.transpose(post).astype(jnp.bfloat16)
    for h in range(2):
        cols = slice(h * HALF, (h + 1) * HALF)
        back = [
            jnp.dot(
                weights,
                img_ref[:, h, part, :, :HALF].reshape(128, HALF),
                preferred_element_type=jnp.float32,
            )
            for part in range(2)
        ]
        sums = [jnp.zeros((8, HALF), jnp.float32) for both in range(4)]
        for t in range(SHIFTS):
            cos, sin = cos_ref[t : t + 1, cols], sin_ref[t : t + 1, cols]
            for e in range(2):
                rows = slice(e * LANES + 8 * t, e * LANES + 8 * t + 8)
                back_re, back_im = back[0][rows], back[1][rows]
                sums[2 * e] += back_re * cos - back_im * sin
                sums[2 * e + 1] += back_im * cos + back_re * sin
        for part in range(2):
            low, high = sums[part].astype(jnp.bfloat16), sums[2 + part].astype(jnp.bfloat16)
            out0_ref[part, :, cols] = jnp.where(straight, low, high)
            out1_ref[part, :, cols] = jnp.where(straight, high, low)
    lane = iota((8, LANES), 1)
    masses = []
    for e in range(2):
        mine = (lane >= MASS) & (lane < MASS + 3)
        mass = jnp.sum(jnp.where(mine, extra[:, e * LANES : (e + 1) * LANES], 0.0), axis=1, keepdims=True)
        row = jnp.zeros((8, LANES), jnp.float32)
        for number, piece in enumerate(pieces_of(mass)):
            row = jnp.where(lane == number, piece, row)
        masses.append(row.astype(jnp.bfloat16))
    for part in range(2):
        out0_ref[part, :, PIXELS:] = jnp.where(straight, masses[0], masses[1])
        out1_ref[part, :, PIXELS:] = jnp.where(straight, masses[1], masses[0])


def final_kernel(first_ref, second_ref, out_ref):
    extra = first_ref[0, :, PIXELS:].astype(jnp.float32) + second_ref[0, :, PIXELS:].astype(jnp.float32)
    mass = jnp.sum(extra, axis=1, keepdims=True)
    for part in range(2):
        both = first_ref[part, :, :PIXELS].astype(jnp.float32) + second_ref[part, :, :PIXELS].astype(jnp.float32)
        out_ref[part] = both / (mass + 1.0)


def call(kernel, shapes, args, scratch=(), scalars=0):
    in_vmem = [pl.BlockSpec(memory_space=pltpu.VMEM)] * (len(args) - scalars)
    in_smem = [pl.BlockSpec(memory_space=pltpu.SMEM)] * scalars
    out = [jax.ShapeDtypeStruct(shape, dtype) for shape, dtype in shapes]
    return pl.pallas_call(
        kernel,
        out_shape=out,
        in_specs=in_vmem + in_smem,
        out_specs=[pl.BlockSpec(memory_space=pltpu.VMEM)] * len(out),
        scratch_shapes=list(scratch),
        compiler_params=pltpu.CompilerParams(vmem_limit_bytes=32 << 20),
    )(*args)


def swap(operand, axes):
    return lax.all_to_all(operand, axes, 0, 0, tiled=True)


def local(images, references, precision, shifts, labels, log_prior):
    y, zh, c, zl, xh, xl = (lax.axis_index(name) for name in ALL)
    half = zh.astype(jnp.int32)[None]
    (sent,) = call(image_kernel, [((16, 2, 16, HALF + LANES), jnp.bfloat16)], (images, precision[None]))
    units = swap(sent, SPACE).reshape(8, 2, 2, 16, HALF + LANES)
    (low,) = call(ref_kernel, [((2, 8, PIXELS + LANES), jnp.bfloat16)], (references, labels[None]))
    refs = [lax.ppermute(low, ALL, route) for route in routes(True)]
    tags = [ref[:1, :, PIXELS:] for ref in refs]
    cosine, sine = phases(shifts, zl * 2 + xh)
    (cross,) = call(
        cross_kernel,
        [((16, 8, 2 * LANES), jnp.float32)],
        (units, *refs, cosine, sine, half),
        [pltpu.VMEM((2, 2 * LANES, PIXELS), jnp.bfloat16)],
        scalars=1,
    )
    scores, stats = call(
        score_kernel,
        [((8, 2 * LANES), jnp.float32), ((16, 8, LANES), jnp.float32)],
        (swap(cross, BLOCK), *tags, log_prior, half),
        scalars=2,
    )
    (post,) = call(post_kernel, [((16, 8, 2 * LANES), jnp.bfloat16)], (swap(stats, SPACE), scores))
    posts = swap(post, BLOCK)
    partial = call(
        back_kernel,
        [((2, 8, PIXELS + LANES), jnp.bfloat16)] * 2,
        (posts, units, cosine, sine, half),
        scalars=1,
    )
    first, second = [lax.ppermute(part, ALL, route) for part, route in zip(partial, routes(False), strict=True)]
    (new_refs,) = call(final_kernel, [((2, 8, PIXELS), jnp.float32)], (first, second))
    mine = lax.dynamic_slice_in_dim(posts, (y * 2 + c) * 2, 2, 0).reshape(16, 2 * LANES)
    shares = mine[:, CLASS : CLASS + 3 * CLASSES].astype(jnp.float32).reshape(16, 3, CLASSES)
    class_post = jnp.sum(shares, axis=1)
    return new_refs, class_post


def solution(mesh):
    whole = Mesh(mesh.devices.reshape(tuple(SIZES.values())), ALL)
    return jax.shard_map(
        local,
        mesh=whole,
        in_specs=(P(None, IMG, REF), P(None, REF, IMG), P(IMG), P(), P(REF), P()),
        out_specs=(P(None, REF, IMG), P(IMG, None)),
        check_vma=False,
    )
```

```python
import itertools
import math

import jax
import jax.numpy as jnp
from jax import lax
from jax.experimental import pallas as pl
from jax.experimental.pallas import tpu as pltpu
from jax.sharding import Mesh
from jax.sharding import PartitionSpec as P

ROWS = 256
COLS = 128
SHIFTS = 12
CLASSES = 4
LANES = 128
USED = SHIFTS * 8
MASS = USED
CLASS = USED + 4
PIXELS = 2048
HALF = 1024
SIZES = {"y": 4, "zh": 2, "c": 2, "zl": 8, "xh": 2, "xl": 2}
ALL = tuple(SIZES)
IMG = ("y", "zh", "c")
REF = ("zl", "xh", "xl")
SPACE = ("y", "c", "xl")
BLOCK = ("zl", "xh")


def place(*coords):
    number = 0
    for size, coord in zip(SIZES.values(), coords, strict=True):
        number = number * size + coord
    return number


def routes(inward):
    made = []
    for r in range(2):
        pairs = []
        for y, zh, c, zl, xh, xl in itertools.product(*(range(size) for size in SIZES.values())):
            work = place(y, zh, c, zl, xh, xl)
            home = place(zl // 2, zl % 2, xh, 2 * y + c, r ^ zh, xl)
            pairs.append((home, work) if inward else (work, home))
        made.append(pairs)
    return made


def phases(shifts, block):
    index = block * PIXELS + jnp.arange(PIXELS, dtype=jnp.int32)
    freq_y = (index // COLS - ROWS // 2).astype(jnp.float32)
    freq_x = (index % COLS).astype(jnp.float32)
    shift_x = shifts[:, 0].astype(jnp.float32)[:, None]
    shift_y = shifts[:, 1].astype(jnp.float32)[:, None]
    angles = 2.0 * math.pi / ROWS * (freq_x[None, :] * shift_x + freq_y[None, :] * shift_y)
    return jnp.cos(angles), jnp.sin(angles)


def iota(shape, axis):
    return lax.broadcasted_iota(jnp.int32, shape, axis)


def own_lanes():
    lane = iota((8, LANES), 1)
    return (lane % 8 == iota((8, LANES), 0)) & (lane < USED)


def as_row(column):
    return jnp.sum(jnp.where(own_lanes(), column, 0.0), axis=0, keepdims=True)


def pieces_of(value):
    first = value.astype(jnp.bfloat16).astype(jnp.float32)
    second = (value - first).astype(jnp.bfloat16).astype(jnp.float32)
    return first, second, value - first - second


def image_kernel(img_ref, precision_ref, out_ref):
    low = img_ref[...].astype(jnp.bfloat16)
    precision = jnp.sum(
        jnp.where(iota((16, 16), 0) == iota((16, 16), 1), precision_ref[...], 0.0), axis=1, keepdims=True
    )
    first, second, third = pieces_of(precision)
    lane = iota((16, LANES), 1)
    pieces = jnp.where(lane == 0, first, jnp.where(lane == 1, second, jnp.where(lane == 2, third, 0.0)))
    pieces = pieces.astype(jnp.bfloat16)
    for copy in range(16):
        out_ref[copy, :, :, :HALF] = low
        out_ref[copy, 0, :, HALF:] = pieces
        out_ref[copy, 1, :, HALF:] = pieces


def ref_kernel(ref_ref, label_ref, out_ref):
    out_ref[:, :, :PIXELS] = ref_ref[...].astype(jnp.bfloat16)
    label = label_ref[...].astype(jnp.float32)
    label = jnp.sum(jnp.where(iota((8, 8), 0) == iota((8, 8), 1), label, 0.0), axis=1, keepdims=True)
    label = jnp.broadcast_to(label, (8, LANES)).astype(jnp.bfloat16)
    out_ref[0, :, PIXELS:] = label
    out_ref[1, :, PIXELS:] = label


def rotate_kernel(ref0_ref, ref1_ref, cos_ref, sin_ref, zh_ref, shifted, half_ref, label_ref):
    straight = zh_ref[0] == 0
    ref0 = ref0_ref[...].astype(jnp.float32)
    ref1 = ref1_ref[...].astype(jnp.float32)
    for e in range(2):
        ref = jnp.where(straight, ref0, ref1) if e == 0 else jnp.where(straight, ref1, ref0)
        re, im = ref[0, :, :PIXELS], ref[1, :, :PIXELS]
        label_ref[:, e * LANES : (e + 1) * LANES] = as_row(ref[0, :, PIXELS:])
        energy = jnp.sum(re * re + im * im, axis=1, keepdims=True)
        half_ref[:, e * LANES : (e + 1) * LANES] = as_row(0.5 * energy)
        for pair in range(SHIFTS // 2):
            rot_re, rot_im = [], []
            for t in (2 * pair, 2 * pair + 1):
                cos, sin = cos_ref[t : t + 1, :], sin_ref[t : t + 1, :]
                rot_re.append(re * cos + im * sin)
                rot_im.append(im * cos - re * sin)
            rows = slice(e * LANES + 16 * pair, e * LANES + 16 * pair + 16)
            shifted[0, rows, :] = jnp.concatenate(rot_re, axis=0).astype(jnp.bfloat16)
            shifted[1, rows, :] = jnp.concatenate(rot_im, axis=0).astype(jnp.bfloat16)
        spare = slice(e * LANES + USED, (e + 1) * LANES)
        shifted[:, spare, :] = jnp.zeros((2, LANES - USED, PIXELS), jnp.bfloat16)


def cross_kernel(img_ref, shifted, half_ref, out_ref):
    total = jnp.zeros((128, 2 * LANES), jnp.float32)
    for h in range(2):
        for part in range(2):
            total += lax.dot_general(
                img_ref[:, h, part, :, :HALF].reshape(128, HALF),
                shifted[part, :, h * HALF : (h + 1) * HALF],
                (((1,), (1,)), ((), ())),
                preferred_element_type=jnp.float32,
            )
    pieces = img_ref[:, 0, 0, :, HALF:].reshape(128, LANES).astype(jnp.float32)
    precision = jnp.sum(pieces, axis=1, keepdims=True)
    out_ref[...] = (precision * (total - half_ref[...])).reshape(16, 8, 2 * LANES)


def score_kernel(got_ref, label_ref, prior_ref, score_ref, out_ref):
    labels = label_ref[...]
    prior = jnp.zeros((1, 2 * LANES), jnp.float32)
    for k in range(CLASSES):
        prior = jnp.where(labels == k, prior_ref[k], prior)
    scores = jnp.sum(got_ref[...], axis=0) + prior
    scores = jnp.where(iota((8, 2 * LANES), 1) % LANES < USED, scores, -jnp.inf)
    score_ref[...] = scores
    top = jnp.max(scores, axis=1, keepdims=True)
    weights = jnp.exp(scores - top)
    lane = iota((8, LANES), 1)
    stats = jnp.where(lane == 0, top, 0.0)
    for k in range(CLASSES):
        mass = jnp.sum(jnp.where(labels == k, weights, 0.0), axis=1, keepdims=True)
        stats = jnp.where(lane == k + 1, mass, stats)
    out_ref[...] = jnp.broadcast_to(stats[None], (16, 8, LANES))


def post_kernel(got_ref, score_ref, out_ref):
    got = got_ref[...]
    tops = got[:, :, 0:1]
    top = jnp.max(tops, axis=0)
    lane = iota((8, LANES), 1)
    sums = jnp.sum(got * jnp.exp(tops - top[None]), axis=0)
    sums = jnp.where((lane > 0) & (lane <= CLASSES), sums, 0.0)
    total = jnp.sum(sums, axis=1, keepdims=True)
    classes = pieces_of(sums / total)
    post = jnp.exp(score_ref[...] - top) / total
    mass_row = jnp.sum(post, axis=0, keepdims=True)
    for e in range(2):
        half = slice(e * LANES, (e + 1) * LANES)
        mass = jnp.sum(jnp.where(own_lanes(), mass_row[:, half], 0.0), axis=1, keepdims=True)
        message = jnp.where(lane < USED, post[:, half], 0.0)
        for number, piece in enumerate(pieces_of(mass)):
            message = jnp.where(lane == MASS + number, piece, message)
        if e == 0:
            for number, piece in enumerate(classes):
                message += pltpu.roll(piece, CLASS + CLASSES * number - 1, 1)
        out_ref[:, :, half] = jnp.broadcast_to(message.astype(jnp.bfloat16)[None], (16, 8, LANES))


def back_kernel(got_ref, img_ref, cos_ref, sin_ref, zh_ref, out0_ref, out1_ref):
    straight = zh_ref[0] == 0
    got = got_ref[...].astype(jnp.float32)
    extra = jnp.sum(got, axis=0)
    post = got.reshape(128, 2 * LANES)
    post = jnp.where(iota((128, 2 * LANES), 1) % LANES < USED, post, 0.0)
    weights = jnp.transpose(post).astype(jnp.bfloat16)
    for h in range(2):
        cols = slice(h * HALF, (h + 1) * HALF)
        back = [
            jnp.dot(
                weights,
                img_ref[:, h, part, :, :HALF].reshape(128, HALF),
                preferred_element_type=jnp.float32,
            )
            for part in range(2)
        ]
        sums = [jnp.zeros((8, HALF), jnp.float32) for both in range(4)]
        for t in range(SHIFTS):
            cos, sin = cos_ref[t : t + 1, cols], sin_ref[t : t + 1, cols]
            for e in range(2):
                rows = slice(e * LANES + 8 * t, e * LANES + 8 * t + 8)
                back_re, back_im = back[0][rows], back[1][rows]
                sums[2 * e] += back_re * cos - back_im * sin
                sums[2 * e + 1] += back_im * cos + back_re * sin
        for part in range(2):
            low, high = sums[part].astype(jnp.bfloat16), sums[2 + part].astype(jnp.bfloat16)
            out0_ref[part, :, cols] = jnp.where(straight, low, high)
            out1_ref[part, :, cols] = jnp.where(straight, high, low)
    lane = iota((8, LANES), 1)
    masses = []
    for e in range(2):
        mine = (lane >= MASS) & (lane < MASS + 3)
        mass = jnp.sum(jnp.where(mine, extra[:, e * LANES : (e + 1) * LANES], 0.0), axis=1, keepdims=True)
        row = jnp.zeros((8, LANES), jnp.float32)
        for number, piece in enumerate(pieces_of(mass)):
            row = jnp.where(lane == number, piece, row)
        masses.append(row.astype(jnp.bfloat16))
    for part in range(2):
        out0_ref[part, :, PIXELS:] = jnp.where(straight, masses[0], masses[1])
        out1_ref[part, :, PIXELS:] = jnp.where(straight, masses[1], masses[0])


def final_kernel(first_ref, second_ref, out_ref):
    extra = first_ref[0, :, PIXELS:].astype(jnp.float32) + second_ref[0, :, PIXELS:].astype(jnp.float32)
    mass = jnp.sum(extra, axis=1, keepdims=True)
    for part in range(2):
        both = first_ref[part, :, :PIXELS].astype(jnp.float32) + second_ref[part, :, :PIXELS].astype(jnp.float32)
        out_ref[part] = both / (mass + 1.0)


def call(kernel, shapes, args, scratch=(), scalars=0, cost=None):
    in_vmem = [pl.BlockSpec(memory_space=pltpu.VMEM)] * (len(args) - scalars)
    in_smem = [pl.BlockSpec(memory_space=pltpu.SMEM)] * scalars
    out = [jax.ShapeDtypeStruct(shape, dtype) for shape, dtype in shapes]
    return pl.pallas_call(
        kernel,
        out_shape=out,
        in_specs=in_vmem + in_smem,
        out_specs=[pl.BlockSpec(memory_space=pltpu.VMEM)] * len(out),
        scratch_shapes=list(scratch),
        compiler_params=pltpu.CompilerParams(vmem_limit_bytes=8 << 20),
        cost_estimate=cost,
    )(*args)


def swap(operand, axes):
    return lax.all_to_all(operand, axes, 0, 0, tiled=True)


def local(images, references, precision, shifts, labels, log_prior):
    y, zh, c, zl, xh, xl = (lax.axis_index(name) for name in ALL)
    half = zh.astype(jnp.int32)[None]
    (low,) = call(ref_kernel, [((2, 8, PIXELS + LANES), jnp.bfloat16)], (references, labels[None]))
    refs = [lax.ppermute(low, ALL, route) for route in routes(True)]
    (sent,) = call(image_kernel, [((16, 2, 16, HALF + LANES), jnp.bfloat16)], (images, precision[None]))
    units = swap(sent, SPACE).reshape(8, 2, 2, 16, HALF + LANES)
    cosine, sine = phases(shifts, zl * 2 + xh)
    shifted, energies, tags = call(
        rotate_kernel,
        [((2, 2 * LANES, PIXELS), jnp.bfloat16), ((1, 2 * LANES), jnp.float32), ((1, 2 * LANES), jnp.float32)],
        (*refs, cosine, sine, half),
        scalars=1,
        cost=pl.CostEstimate(flops=60_000_000_000, transcendentals=0, bytes_accessed=8 << 20),
    )
    (cross,) = call(cross_kernel, [((16, 8, 2 * LANES), jnp.float32)], (units, shifted, energies))
    scores, stats = call(
        score_kernel,
        [((8, 2 * LANES), jnp.float32), ((16, 8, LANES), jnp.float32)],
        (swap(cross, BLOCK), tags, log_prior),
        scalars=1,
    )
    (post,) = call(post_kernel, [((16, 8, 2 * LANES), jnp.bfloat16)], (swap(stats, SPACE), scores))
    posts = swap(post, BLOCK)
    partial = call(
        back_kernel,
        [((2, 8, PIXELS + LANES), jnp.bfloat16)] * 2,
        (posts, units, cosine, sine, half),
        scalars=1,
    )
    first, second = [lax.ppermute(part, ALL, route) for part, route in zip(partial, routes(False), strict=True)]
    (new_refs,) = call(final_kernel, [((2, 8, PIXELS), jnp.float32)], (first, second))
    mine = lax.dynamic_slice_in_dim(posts, (y * 2 + c) * 2, 2, 0).reshape(16, 2 * LANES)
    shares = mine[:, CLASS : CLASS + 3 * CLASSES].astype(jnp.float32).reshape(16, 3, CLASSES)
    class_post = jnp.sum(shares, axis=1)
    return new_refs, class_post


def solution(mesh):
    whole = Mesh(mesh.devices.reshape(tuple(SIZES.values())), ALL)
    return jax.shard_map(
        local,
        mesh=whole,
        in_specs=(P(None, IMG, REF), P(None, REF, IMG), P(IMG), P(), P(REF), P()),
        out_specs=(P(None, REF, IMG), P(IMG, None)),
        check_vma=False,
    )
```

```python
import itertools
import math

import jax
import jax.numpy as jnp
from jax import lax
from jax.experimental import pallas as pl
from jax.experimental.pallas import tpu as pltpu
from jax.sharding import Mesh
from jax.sharding import PartitionSpec as P

ROWS = 256
COLS = 128
SHIFTS = 12
CLASSES = 4
LANES = 128
USED = SHIFTS * 8
MASS = USED
CLASS = USED + 4
PIXELS = 2048
HALF = 1024
SIZES = {"y": 4, "zh": 2, "c": 2, "zl": 8, "xh": 2, "xl": 2}
ALL = tuple(SIZES)
IMG = ("y", "zh", "c")
REF = ("zl", "xh", "xl")
SPACE = ("y", "c", "xl")
BLOCK = ("zl", "xh")


def place(*coords):
    number = 0
    for size, coord in zip(SIZES.values(), coords, strict=True):
        number = number * size + coord
    return number


def routes(inward):
    made = []
    for r in range(2):
        pairs = []
        for y, zh, c, zl, xh, xl in itertools.product(*(range(size) for size in SIZES.values())):
            work = place(y, zh, c, zl, xh, xl)
            home = place(zl // 2, zl % 2, xh, 2 * y + c, r ^ zh, xl)
            pairs.append((home, work) if inward else (work, home))
        made.append(pairs)
    return made


def phases(shifts, block):
    index = block * PIXELS + jnp.arange(PIXELS, dtype=jnp.int32)
    freq_y = (index // COLS - ROWS // 2).astype(jnp.float32)
    freq_x = (index % COLS).astype(jnp.float32)
    shift_x = shifts[:, 0].astype(jnp.float32)[:, None]
    shift_y = shifts[:, 1].astype(jnp.float32)[:, None]
    angles = 2.0 * math.pi / ROWS * (freq_x[None, :] * shift_x + freq_y[None, :] * shift_y)
    return jnp.cos(angles), jnp.sin(angles)


def iota(shape, axis):
    return lax.broadcasted_iota(jnp.int32, shape, axis)


def own_lanes():
    lane = iota((8, LANES), 1)
    return (lane % 8 == iota((8, LANES), 0)) & (lane < USED)


def as_row(column):
    return jnp.sum(jnp.where(own_lanes(), column, 0.0), axis=0, keepdims=True)


def pieces_of(value):
    first = value.astype(jnp.bfloat16).astype(jnp.float32)
    second = (value - first).astype(jnp.bfloat16).astype(jnp.float32)
    return first, second, value - first - second


def image_kernel(img_ref, precision_ref, out_ref):
    low = img_ref[...].astype(jnp.bfloat16)
    precision = jnp.sum(
        jnp.where(iota((16, 16), 0) == iota((16, 16), 1), precision_ref[...], 0.0), axis=1, keepdims=True
    )
    first, second, third = pieces_of(precision)
    lane = iota((16, LANES), 1)
    pieces = jnp.where(lane == 0, first, jnp.where(lane == 1, second, jnp.where(lane == 2, third, 0.0)))
    pieces = pieces.astype(jnp.bfloat16)
    for copy in range(16):
        out_ref[copy, :, :, :HALF] = low
        out_ref[copy, 0, :, HALF:] = pieces
        out_ref[copy, 1, :, HALF:] = pieces


def ref_kernel(ref_ref, label_ref, out_ref):
    out_ref[:, :, :PIXELS] = ref_ref[...].astype(jnp.bfloat16)
    label = label_ref[...].astype(jnp.float32)
    label = jnp.sum(jnp.where(iota((8, 8), 0) == iota((8, 8), 1), label, 0.0), axis=1, keepdims=True)
    label = jnp.broadcast_to(label, (8, LANES)).astype(jnp.bfloat16)
    out_ref[0, :, PIXELS:] = label
    out_ref[1, :, PIXELS:] = label


def cross_kernel(img_ref, ref_ref, cos_ref, sin_ref, zh_ref, out_ref, shifted):
    straight = zh_ref[0] == 0
    ref0 = ref_ref[0, :, :, :PIXELS].astype(jnp.float32)
    ref1 = ref_ref[1, :, :, :PIXELS].astype(jnp.float32)
    halves = []
    for e in range(2):
        ref = jnp.where(straight, ref0, ref1) if e == 0 else jnp.where(straight, ref1, ref0)
        re, im = ref[0], ref[1]
        halves.append(as_row(0.5 * jnp.sum(re * re + im * im, axis=1, keepdims=True)))
        for pair in range(SHIFTS // 2):
            rot_re, rot_im = [], []
            for t in (2 * pair, 2 * pair + 1):
                cos, sin = cos_ref[t : t + 1, :], sin_ref[t : t + 1, :]
                rot_re.append(re * cos + im * sin)
                rot_im.append(im * cos - re * sin)
            rows = slice(e * LANES + 16 * pair, e * LANES + 16 * pair + 16)
            shifted[0, rows, :] = jnp.concatenate(rot_re, axis=0).astype(jnp.bfloat16)
            shifted[1, rows, :] = jnp.concatenate(rot_im, axis=0).astype(jnp.bfloat16)
        spare = slice(e * LANES + USED, (e + 1) * LANES)
        shifted[:, spare, :] = jnp.zeros((2, LANES - USED, PIXELS), jnp.bfloat16)
    total = jnp.zeros((128, 2 * LANES), jnp.float32)
    for h in range(2):
        for part in range(2):
            total += lax.dot_general(
                img_ref[:, h, part, :, :HALF].reshape(128, HALF),
                shifted[part, :, h * HALF : (h + 1) * HALF],
                (((1,), (1,)), ((), ())),
                preferred_element_type=jnp.float32,
            )
    pieces = img_ref[:, 0, 0, :, HALF:].reshape(128, LANES).astype(jnp.float32)
    precision = jnp.sum(pieces, axis=1, keepdims=True)
    scaled = precision * (total - jnp.concatenate(halves, axis=1))
    out_ref[...] = scaled.reshape(16, 8, 2 * LANES)


def label_rows(tag_ref, straight):
    first = tag_ref[0, 0].astype(jnp.float32)
    second = tag_ref[1, 0].astype(jnp.float32)
    low, high = jnp.where(straight, first, second), jnp.where(straight, second, first)
    return jnp.concatenate([as_row(low), as_row(high)], axis=1)


def score_kernel(got_ref, tag_ref, prior_ref, zh_ref, score_ref, out_ref):
    labels = label_rows(tag_ref, zh_ref[0] == 0)
    prior = jnp.zeros((1, 2 * LANES), jnp.float32)
    for k in range(CLASSES):
        prior = jnp.where(labels == k, prior_ref[k], prior)
    scores = jnp.sum(got_ref[...], axis=0) + prior
    scores = jnp.where(iota((8, 2 * LANES), 1) % LANES < USED, scores, -jnp.inf)
    score_ref[...] = scores
    top = jnp.max(scores, axis=1, keepdims=True)
    weights = jnp.exp(scores - top)
    lane = iota((8, LANES), 1)
    stats = jnp.where(lane == 0, top, 0.0)
    for k in range(CLASSES):
        mass = jnp.sum(jnp.where(labels == k, weights, 0.0), axis=1, keepdims=True)
        stats = jnp.where(lane == k + 1, mass, stats)
    out_ref[...] = jnp.broadcast_to(stats[None], (16, 8, LANES))


def post_kernel(got_ref, score_ref, out_ref):
    got = got_ref[...]
    tops = got[:, :, 0:1]
    top = jnp.max(tops, axis=0)
    lane = iota((8, LANES), 1)
    sums = jnp.sum(got * jnp.exp(tops - top[None]), axis=0)
    sums = jnp.where((lane > 0) & (lane <= CLASSES), sums, 0.0)
    total = jnp.sum(sums, axis=1, keepdims=True)
    classes = pieces_of(sums / total)
    post = jnp.exp(score_ref[...] - top) / total
    mass_row = jnp.sum(post, axis=0, keepdims=True)
    for e in range(2):
        half = slice(e * LANES, (e + 1) * LANES)
        mass = jnp.sum(jnp.where(own_lanes(), mass_row[:, half], 0.0), axis=1, keepdims=True)
        message = jnp.where(lane < USED, post[:, half], 0.0)
        for number, piece in enumerate(pieces_of(mass)):
            message = jnp.where(lane == MASS + number, piece, message)
        if e == 0:
            for number, piece in enumerate(classes):
                message += pltpu.roll(piece, CLASS + CLASSES * number - 1, 1)
        out_ref[:, :, half] = jnp.broadcast_to(message.astype(jnp.bfloat16)[None], (16, 8, LANES))


def back_kernel(got_ref, img_ref, cos_ref, sin_ref, zh_ref, out0_ref, out1_ref):
    straight = zh_ref[0] == 0
    got = got_ref[...].astype(jnp.float32)
    extra = jnp.sum(got, axis=0)
    post = got.reshape(128, 2 * LANES)
    post = jnp.where(iota((128, 2 * LANES), 1) % LANES < USED, post, 0.0)
    weights = jnp.transpose(post).astype(jnp.bfloat16)
    for h in range(2):
        cols = slice(h * HALF, (h + 1) * HALF)
        back = [
            jnp.dot(
                weights,
                img_ref[:, h, part, :, :HALF].reshape(128, HALF),
                preferred_element_type=jnp.float32,
            )
            for part in range(2)
        ]
        sums = [jnp.zeros((8, HALF), jnp.float32) for both in range(4)]
        for t in range(SHIFTS):
            cos, sin = cos_ref[t : t + 1, cols], sin_ref[t : t + 1, cols]
            for e in range(2):
                rows = slice(e * LANES + 8 * t, e * LANES + 8 * t + 8)
                back_re, back_im = back[0][rows], back[1][rows]
                sums[2 * e] += back_re * cos - back_im * sin
                sums[2 * e + 1] += back_im * cos + back_re * sin
        for part in range(2):
            low, high = sums[part].astype(jnp.bfloat16), sums[2 + part].astype(jnp.bfloat16)
            out0_ref[part, :, cols] = jnp.where(straight, low, high)
            out1_ref[part, :, cols] = jnp.where(straight, high, low)
    lane = iota((8, LANES), 1)
    masses = []
    for e in range(2):
        mine = (lane >= MASS) & (lane < MASS + 3)
        mass = jnp.sum(jnp.where(mine, extra[:, e * LANES : (e + 1) * LANES], 0.0), axis=1, keepdims=True)
        row = jnp.zeros((8, LANES), jnp.float32)
        for number, piece in enumerate(pieces_of(mass)):
            row = jnp.where(lane == number, piece, row)
        masses.append(row.astype(jnp.bfloat16))
    for part in range(2):
        out0_ref[part, :, PIXELS:] = jnp.where(straight, masses[0], masses[1])
        out1_ref[part, :, PIXELS:] = jnp.where(straight, masses[1], masses[0])


def final_kernel(first_ref, second_ref, out_ref):
    extra = first_ref[0, :, PIXELS:].astype(jnp.float32) + second_ref[0, :, PIXELS:].astype(jnp.float32)
    mass = jnp.sum(extra, axis=1, keepdims=True)
    for part in range(2):
        both = first_ref[part, :, :PIXELS].astype(jnp.float32) + second_ref[part, :, :PIXELS].astype(jnp.float32)
        out_ref[part] = both / (mass + 1.0)


def call(kernel, shapes, args, scratch=(), scalars=0):
    in_vmem = [pl.BlockSpec(memory_space=pltpu.VMEM)] * (len(args) - scalars)
    in_smem = [pl.BlockSpec(memory_space=pltpu.SMEM)] * scalars
    out = [jax.ShapeDtypeStruct(shape, dtype) for shape, dtype in shapes]
    return pl.pallas_call(
        kernel,
        out_shape=out,
        in_specs=in_vmem + in_smem,
        out_specs=[pl.BlockSpec(memory_space=pltpu.VMEM)] * len(out),
        scratch_shapes=list(scratch),
        compiler_params=pltpu.CompilerParams(vmem_limit_bytes=32 << 20),
    )(*args)


def swap(operand, axes):
    return lax.all_to_all(operand, axes, 0, 0, tiled=True)


def local(images, references, precision, shifts, labels, log_prior):
    y, zh, c, zl, xh, xl = (lax.axis_index(name) for name in ALL)
    half = zh.astype(jnp.int32)[None]
    (sent,) = call(image_kernel, [((16, 2, 16, HALF + LANES), jnp.bfloat16)], (images, precision[None]))
    units = swap(sent, SPACE).reshape(8, 2, 2, 16, HALF + LANES)
    (low,) = call(ref_kernel, [((2, 8, PIXELS + LANES), jnp.bfloat16)], (references, labels[None]))
    other = lax.ppermute(low, "xh", [(0, 1), (1, 0)])
    refs = lax.ppermute(jnp.stack([low, other]), ALL, routes(True)[0])
    tags = refs[:, :1, :, PIXELS:]
    cosine, sine = phases(shifts, zl * 2 + xh)
    (cross,) = call(
        cross_kernel,
        [((16, 8, 2 * LANES), jnp.float32)],
        (units, refs, cosine, sine, half),
        [pltpu.VMEM((2, 2 * LANES, PIXELS), jnp.bfloat16)],
        scalars=1,
    )
    scores, stats = call(
        score_kernel,
        [((8, 2 * LANES), jnp.float32), ((16, 8, LANES), jnp.float32)],
        (swap(cross, BLOCK), tags, log_prior, half),
        scalars=2,
    )
    (post,) = call(post_kernel, [((16, 8, 2 * LANES), jnp.bfloat16)], (swap(stats, SPACE), scores))
    posts = swap(post, BLOCK)
    partial = call(
        back_kernel,
        [((2, 8, PIXELS + LANES), jnp.bfloat16)] * 2,
        (posts, units, cosine, sine, half),
        scalars=1,
    )
    first, second = [lax.ppermute(part, ALL, route) for part, route in zip(partial, routes(False), strict=True)]
    (new_refs,) = call(final_kernel, [((2, 8, PIXELS), jnp.float32)], (first, second))
    mine = lax.dynamic_slice_in_dim(posts, (y * 2 + c) * 2, 2, 0).reshape(16, 2 * LANES)
    shares = mine[:, CLASS : CLASS + 3 * CLASSES].astype(jnp.float32).reshape(16, 3, CLASSES)
    class_post = jnp.sum(shares, axis=1)
    return new_refs, class_post


def solution(mesh):
    whole = Mesh(mesh.devices.reshape(tuple(SIZES.values())), ALL)
    return jax.shard_map(
        local,
        mesh=whole,
        in_specs=(P(None, IMG, REF), P(None, REF, IMG), P(IMG), P(), P(REF), P()),
        out_specs=(P(None, REF, IMG), P(IMG, None)),
        check_vma=False,
    )
```

```python
import itertools
import math

import jax
import jax.numpy as jnp
from jax import lax
from jax.experimental import pallas as pl
from jax.experimental.pallas import tpu as pltpu
from jax.sharding import Mesh
from jax.sharding import PartitionSpec as P

ROWS = 256
COLS = 128
SHIFTS = 12
CLASSES = 4
LANES = 128
USED = SHIFTS * 8
MASS = USED
CLASS = USED + 4
PIXELS = 2048
HALF = 1024
SIZES = {"y": 4, "zh": 2, "c": 2, "zl": 8, "xh": 2, "xl": 2}
ALL = tuple(SIZES)
IMG = ("y", "zh", "c")
REF = ("zl", "xh", "xl")
SPACE = ("y", "c", "xl")
NEAR = ("y", "xl")
BLOCK = ("zl", "xh")


def place(*coords):
    number = 0
    for size, coord in zip(SIZES.values(), coords, strict=True):
        number = number * size + coord
    return number


def routes(inward):
    made = []
    for r in range(2):
        pairs = []
        for y, zh, c, zl, xh, xl in itertools.product(*(range(size) for size in SIZES.values())):
            work = place(y, zh, c, zl, xh, xl)
            home = place(zl // 2, zl % 2, xh, 2 * y + c, r ^ zh, xl)
            pairs.append((home, work) if inward else (work, home))
        made.append(pairs)
    return made


def phases(shifts, block):
    index = block * PIXELS + jnp.arange(PIXELS, dtype=jnp.int32)
    freq_y = (index // COLS - ROWS // 2).astype(jnp.float32)
    freq_x = (index % COLS).astype(jnp.float32)
    shift_x = shifts[:, 0].astype(jnp.float32)[:, None]
    shift_y = shifts[:, 1].astype(jnp.float32)[:, None]
    angles = 2.0 * math.pi / ROWS * (freq_x[None, :] * shift_x + freq_y[None, :] * shift_y)
    return jnp.cos(angles), jnp.sin(angles)


def iota(shape, axis):
    return lax.broadcasted_iota(jnp.int32, shape, axis)


def own_lanes():
    lane = iota((8, LANES), 1)
    return (lane % 8 == iota((8, LANES), 0)) & (lane < USED)


def as_row(column):
    return jnp.sum(jnp.where(own_lanes(), column, 0.0), axis=0, keepdims=True)


def pieces_of(value):
    first = value.astype(jnp.bfloat16).astype(jnp.float32)
    second = (value - first).astype(jnp.bfloat16).astype(jnp.float32)
    return first, second, value - first - second


def image_kernel(img_ref, precision_ref, out_ref):
    low = img_ref[...].astype(jnp.bfloat16)
    precision = jnp.sum(
        jnp.where(iota((16, 16), 0) == iota((16, 16), 1), precision_ref[...], 0.0), axis=1, keepdims=True
    )
    first, second, third = pieces_of(precision)
    lane = iota((16, LANES), 1)
    pieces = jnp.where(lane == 0, first, jnp.where(lane == 1, second, jnp.where(lane == 2, third, 0.0)))
    pieces = pieces.astype(jnp.bfloat16)
    for copy in range(8):
        out_ref[copy, :, :, :HALF] = low
        out_ref[copy, 0, :, HALF:] = pieces
        out_ref[copy, 1, :, HALF:] = pieces


def ref_kernel(ref_ref, label_ref, out_ref):
    out_ref[:, :, :PIXELS] = ref_ref[...].astype(jnp.bfloat16)
    label = label_ref[...].astype(jnp.float32)
    label = jnp.sum(jnp.where(iota((8, 8), 0) == iota((8, 8), 1), label, 0.0), axis=1, keepdims=True)
    label = jnp.broadcast_to(label, (8, LANES)).astype(jnp.bfloat16)
    out_ref[0, :, PIXELS:] = label
    out_ref[1, :, PIXELS:] = label


def cross_kernel(own_ref, other_ref, ref0_ref, ref1_ref, cos_ref, sin_ref, zh_ref, c_ref, out_ref, shifted):
    straight = zh_ref[0] == 0
    ref0 = ref0_ref[:, :, :PIXELS].astype(jnp.float32)
    ref1 = ref1_ref[:, :, :PIXELS].astype(jnp.float32)
    halves = []
    for e in range(2):
        ref = jnp.where(straight, ref0, ref1) if e == 0 else jnp.where(straight, ref1, ref0)
        re, im = ref[0], ref[1]
        halves.append(as_row(0.5 * jnp.sum(re * re + im * im, axis=1, keepdims=True)))
        for pair in range(SHIFTS // 2):
            rot_re, rot_im = [], []
            for t in (2 * pair, 2 * pair + 1):
                cos, sin = cos_ref[t : t + 1, :], sin_ref[t : t + 1, :]
                rot_re.append(re * cos + im * sin)
                rot_im.append(im * cos - re * sin)
            rows = slice(e * LANES + 16 * pair, e * LANES + 16 * pair + 16)
            shifted[0, rows, :] = jnp.concatenate(rot_re, axis=0).astype(jnp.bfloat16)
            shifted[1, rows, :] = jnp.concatenate(rot_im, axis=0).astype(jnp.bfloat16)
        spare = slice(e * LANES + USED, (e + 1) * LANES)
        shifted[:, spare, :] = jnp.zeros((2, LANES - USED, PIXELS), jnp.bfloat16)
    half = jnp.concatenate(halves, axis=1)
    for img_ref, chip in ((own_ref, c_ref[0]), (other_ref, 1 - c_ref[0])):
        total = jnp.zeros((64, 2 * LANES), jnp.float32)
        for h in range(2):
            for part in range(2):
                total += lax.dot_general(
                    img_ref[:, h, part, :, :HALF].reshape(64, HALF),
                    shifted[part, :, h * HALF : (h + 1) * HALF],
                    (((1,), (1,)), ((), ())),
                    preferred_element_type=jnp.float32,
                )
        pieces = img_ref[:, 0, 0, :, HALF:].reshape(64, LANES).astype(jnp.float32)
        precision = jnp.sum(pieces, axis=1, keepdims=True)
        out_ref[pl.ds(chip * 8, 8)] = (precision * (total - half)).reshape(8, 8, 2 * LANES)


def label_rows(ref0_ref, ref1_ref, straight):
    first = ref0_ref[0].astype(jnp.float32)
    second = ref1_ref[0].astype(jnp.float32)
    low, high = jnp.where(straight, first, second), jnp.where(straight, second, first)
    return jnp.concatenate([as_row(low), as_row(high)], axis=1)


def score_kernel(got_ref, ref0_ref, ref1_ref, prior_ref, zh_ref, score_ref, out_ref):
    labels = label_rows(ref0_ref, ref1_ref, zh_ref[0] == 0)
    prior = jnp.zeros((1, 2 * LANES), jnp.float32)
    for k in range(CLASSES):
        prior = jnp.where(labels == k, prior_ref[k], prior)
    scores = jnp.sum(got_ref[...], axis=0) + prior
    scores = jnp.where(iota((8, 2 * LANES), 1) % LANES < USED, scores, -jnp.inf)
    score_ref[...] = scores
    top = jnp.max(scores, axis=1, keepdims=True)
    weights = jnp.exp(scores - top)
    lane = iota((8, LANES), 1)
    stats = jnp.where(lane == 0, top, 0.0)
    for k in range(CLASSES):
        mass = jnp.sum(jnp.where(labels == k, weights, 0.0), axis=1, keepdims=True)
        stats = jnp.where(lane == k + 1, mass, stats)
    out_ref[...] = jnp.broadcast_to(stats[None], (16, 8, LANES))


def post_kernel(got_ref, score_ref, out_ref):
    got = got_ref[...]
    tops = got[:, :, 0:1]
    top = jnp.max(tops, axis=0)
    lane = iota((8, LANES), 1)
    sums = jnp.sum(got * jnp.exp(tops - top[None]), axis=0)
    sums = jnp.where((lane > 0) & (lane <= CLASSES), sums, 0.0)
    total = jnp.sum(sums, axis=1, keepdims=True)
    classes = pieces_of(sums / total)
    post = jnp.exp(score_ref[...] - top) / total
    mass_row = jnp.sum(post, axis=0, keepdims=True)
    for e in range(2):
        half = slice(e * LANES, (e + 1) * LANES)
        mass = jnp.sum(jnp.where(own_lanes(), mass_row[:, half], 0.0), axis=1, keepdims=True)
        message = jnp.where(lane < USED, post[:, half], 0.0)
        for number, piece in enumerate(pieces_of(mass)):
            message = jnp.where(lane == MASS + number, piece, message)
        if e == 0:
            for number, piece in enumerate(classes):
                message += pltpu.roll(piece, CLASS + CLASSES * number - 1, 1)
        out_ref[:, :, half] = jnp.broadcast_to(message.astype(jnp.bfloat16)[None], (16, 8, LANES))


def back_kernel(got_ref, own_ref, other_ref, cos_ref, sin_ref, zh_ref, c_ref, out0_ref, out1_ref):
    straight = zh_ref[0] == 0
    extra = jnp.sum(got_ref[...].astype(jnp.float32), axis=0)
    sides = []
    for img_ref, chip in ((own_ref, c_ref[0]), (other_ref, 1 - c_ref[0])):
        post = got_ref[pl.ds(chip * 8, 8)].astype(jnp.float32).reshape(64, 2 * LANES)
        post = jnp.where(iota((64, 2 * LANES), 1) % LANES < USED, post, 0.0)
        sides.append((img_ref, jnp.transpose(post).astype(jnp.bfloat16)))
    for h in range(2):
        cols = slice(h * HALF, (h + 1) * HALF)
        back = [
            sum(
                jnp.dot(
                    weights,
                    img_ref[:, h, part, :, :HALF].reshape(64, HALF),
                    preferred_element_type=jnp.float32,
                )
                for img_ref, weights in sides
            )
            for part in range(2)
        ]
        sums = [jnp.zeros((8, HALF), jnp.float32) for both in range(4)]
        for t in range(SHIFTS):
            cos, sin = cos_ref[t : t + 1, cols], sin_ref[t : t + 1, cols]
            for e in range(2):
                rows = slice(e * LANES + 8 * t, e * LANES + 8 * t + 8)
                back_re, back_im = back[0][rows], back[1][rows]
                sums[2 * e] += back_re * cos - back_im * sin
                sums[2 * e + 1] += back_im * cos + back_re * sin
        for part in range(2):
            low, high = sums[part].astype(jnp.bfloat16), sums[2 + part].astype(jnp.bfloat16)
            out0_ref[part, :, cols] = jnp.where(straight, low, high)
            out1_ref[part, :, cols] = jnp.where(straight, high, low)
    lane = iota((8, LANES), 1)
    masses = []
    for e in range(2):
        mine = (lane >= MASS) & (lane < MASS + 3)
        mass = jnp.sum(jnp.where(mine, extra[:, e * LANES : (e + 1) * LANES], 0.0), axis=1, keepdims=True)
        row = jnp.zeros((8, LANES), jnp.float32)
        for number, piece in enumerate(pieces_of(mass)):
            row = jnp.where(lane == number, piece, row)
        masses.append(row.astype(jnp.bfloat16))
    for part in range(2):
        out0_ref[part, :, PIXELS:] = jnp.where(straight, masses[0], masses[1])
        out1_ref[part, :, PIXELS:] = jnp.where(straight, masses[1], masses[0])


def final_kernel(first_ref, second_ref, out_ref):
    extra = first_ref[0, :, PIXELS:].astype(jnp.float32) + second_ref[0, :, PIXELS:].astype(jnp.float32)
    mass = jnp.sum(extra, axis=1, keepdims=True)
    for part in range(2):
        both = first_ref[part, :, :PIXELS].astype(jnp.float32) + second_ref[part, :, :PIXELS].astype(jnp.float32)
        out_ref[part] = both / (mass + 1.0)


def call(kernel, shapes, args, scratch=(), scalars=0):
    in_vmem = [pl.BlockSpec(memory_space=pltpu.VMEM)] * (len(args) - scalars)
    in_smem = [pl.BlockSpec(memory_space=pltpu.SMEM)] * scalars
    out = [jax.ShapeDtypeStruct(shape, dtype) for shape, dtype in shapes]
    return pl.pallas_call(
        kernel,
        out_shape=out,
        in_specs=in_vmem + in_smem,
        out_specs=[pl.BlockSpec(memory_space=pltpu.VMEM)] * len(out),
        scratch_shapes=list(scratch),
        compiler_params=pltpu.CompilerParams(vmem_limit_bytes=32 << 20),
    )(*args)


def swap(operand, axes):
    return lax.all_to_all(operand, axes, 0, 0, tiled=True)


def local(images, references, precision, shifts, labels, log_prior):
    y, zh, c, zl, xh, xl = (lax.axis_index(name) for name in ALL)
    half = zh.astype(jnp.int32)[None]
    (sent,) = call(image_kernel, [((8, 2, 16, HALF + LANES), jnp.bfloat16)], (images, precision[None]))
    own = swap(sent, NEAR).reshape(4, 2, 2, 16, HALF + LANES)
    other = lax.ppermute(own, "c", [(0, 1), (1, 0)])
    core = c.astype(jnp.int32)[None]
    (low,) = call(ref_kernel, [((2, 8, PIXELS + LANES), jnp.bfloat16)], (references, labels[None]))
    refs = [lax.ppermute(low, ALL, route) for route in routes(True)]
    tags = [ref[:1, :, PIXELS:] for ref in refs]
    cosine, sine = phases(shifts, zl * 2 + xh)
    (cross,) = call(
        cross_kernel,
        [((16, 8, 2 * LANES), jnp.float32)],
        (own, other, *refs, cosine, sine, half, core),
        [pltpu.VMEM((2, 2 * LANES, PIXELS), jnp.bfloat16)],
        scalars=2,
    )
    scores, stats = call(
        score_kernel,
        [((8, 2 * LANES), jnp.float32), ((16, 8, LANES), jnp.float32)],
        (swap(cross, BLOCK), *tags, log_prior, half),
        scalars=2,
    )
    (post,) = call(post_kernel, [((16, 8, 2 * LANES), jnp.bfloat16)], (swap(stats, SPACE), scores))
    posts = swap(post, BLOCK)
    partial = call(
        back_kernel,
        [((2, 8, PIXELS + LANES), jnp.bfloat16)] * 2,
        (posts, own, other, cosine, sine, half, core),
        scalars=2,
    )
    first, second = [lax.ppermute(part, ALL, route) for part, route in zip(partial, routes(False), strict=True)]
    (new_refs,) = call(final_kernel, [((2, 8, PIXELS), jnp.float32)], (first, second))
    mine = lax.dynamic_slice_in_dim(posts, (c * 4 + y) * 2, 2, 0).reshape(16, 2 * LANES)
    shares = mine[:, CLASS : CLASS + 3 * CLASSES].astype(jnp.float32).reshape(16, 3, CLASSES)
    class_post = jnp.sum(shares, axis=1)
    return new_refs, class_post


def solution(mesh):
    whole = Mesh(mesh.devices.reshape(tuple(SIZES.values())), ALL)
    return jax.shard_map(
        local,
        mesh=whole,
        in_specs=(P(None, IMG, REF), P(None, REF, IMG), P(IMG), P(), P(REF), P()),
        out_specs=(P(None, REF, IMG), P(IMG, None)),
        check_vma=False,
    )
```

```python
import itertools
import math

import jax
import jax.numpy as jnp
from jax import lax
from jax.experimental import pallas as pl
from jax.experimental.pallas import tpu as pltpu
from jax.sharding import Mesh
from jax.sharding import PartitionSpec as P

ROWS = 256
COLS = 128
SHIFTS = 12
CLASSES = 4
LANES = 128
USED = SHIFTS * 8
MASS = USED
CLASS = USED + 4
PIXELS = 2048
HALF = 1024
SIZES = {"y": 4, "zh": 2, "c": 2, "zu": 2, "zv": 4, "xh": 2, "xl": 2}
ALL = tuple(SIZES)
IMG = ("y", "zh", "c")
REF = ("zu", "zv", "xh", "xl")
SPACE = ("zv", "xh", "xl")
BLOCK = IMG
SWAP = [(0, 1), (1, 0)]


def place(*coords):
    number = 0
    for size, coord in zip(SIZES.values(), coords, strict=True):
        number = number * size + coord
    return number


def image_route():
    pairs = []
    for y, zh, c, zu, zv, xh, xl in itertools.product(*(range(size) for size in SIZES.values())):
        work = place(2 * zu + zv // 2, zv % 2, xh, y // 2, 2 * (y % 2) + zh, c, xl)
        pairs.append((place(y, zh, c, zu, zv, xh, xl), work))
    return pairs


IMG_ROUTE = image_route()


def phases(shifts, block):
    index = block * PIXELS + jnp.arange(PIXELS, dtype=jnp.int32)
    freq_y = (index // COLS - ROWS // 2).astype(jnp.float32)
    freq_x = (index % COLS).astype(jnp.float32)
    shift_x = shifts[:, 0].astype(jnp.float32)[:, None]
    shift_y = shifts[:, 1].astype(jnp.float32)[:, None]
    angles = 2.0 * math.pi / ROWS * (freq_x[None, :] * shift_x + freq_y[None, :] * shift_y)
    return jnp.cos(angles), jnp.sin(angles)


def iota(shape, axis):
    return lax.broadcasted_iota(jnp.int32, shape, axis)


def own_lanes():
    lane = iota((8, LANES), 1)
    return (lane % 8 == iota((8, LANES), 0)) & (lane < USED)


def as_row(column):
    return jnp.sum(jnp.where(own_lanes(), column, 0.0), axis=0, keepdims=True)


def pieces_of(value):
    first = value.astype(jnp.bfloat16).astype(jnp.float32)
    second = (value - first).astype(jnp.bfloat16).astype(jnp.float32)
    return first, second, value - first - second


def image_kernel(img_ref, precision_ref, out_ref):
    low = img_ref[...].astype(jnp.bfloat16)
    precision = jnp.sum(
        jnp.where(iota((16, 16), 0) == iota((16, 16), 1), precision_ref[...], 0.0), axis=1, keepdims=True
    )
    first, second, third = pieces_of(precision)
    lane = iota((16, LANES), 1)
    pieces = jnp.where(lane == 0, first, jnp.where(lane == 1, second, jnp.where(lane == 2, third, 0.0)))
    pieces = pieces.astype(jnp.bfloat16)
    out_ref[:, :, :HALF] = low
    out_ref[0, :, HALF:] = pieces
    out_ref[1, :, HALF:] = pieces


def ref_kernel(ref_ref, label_ref, out_ref):
    out_ref[:, :, :PIXELS] = ref_ref[...].astype(jnp.bfloat16)
    label = label_ref[...].astype(jnp.float32)
    label = jnp.sum(jnp.where(iota((8, 8), 0) == iota((8, 8), 1), label, 0.0), axis=1, keepdims=True)
    label = jnp.broadcast_to(label, (8, LANES)).astype(jnp.bfloat16)
    out_ref[0, :, PIXELS:] = label
    out_ref[1, :, PIXELS:] = label


def cross_kernel(img_ref, ref0_ref, ref1_ref, cos_ref, sin_ref, zu_ref, out_ref, shifted):
    straight = zu_ref[0] == 0
    ref0 = ref0_ref[:, :, :PIXELS].astype(jnp.float32)
    ref1 = ref1_ref[:, :, :PIXELS].astype(jnp.float32)
    halves = []
    for e in range(2):
        ref = jnp.where(straight, ref0, ref1) if e == 0 else jnp.where(straight, ref1, ref0)
        re, im = ref[0], ref[1]
        halves.append(as_row(0.5 * jnp.sum(re * re + im * im, axis=1, keepdims=True)))
        for pair in range(SHIFTS // 2):
            rot_re, rot_im = [], []
            for t in (2 * pair, 2 * pair + 1):
                cos, sin = cos_ref[t : t + 1, :], sin_ref[t : t + 1, :]
                rot_re.append(re * cos + im * sin)
                rot_im.append(im * cos - re * sin)
            rows = slice(e * LANES + 16 * pair, e * LANES + 16 * pair + 16)
            shifted[0, rows, :] = jnp.concatenate(rot_re, axis=0).astype(jnp.bfloat16)
            shifted[1, rows, :] = jnp.concatenate(rot_im, axis=0).astype(jnp.bfloat16)
        spare = slice(e * LANES + USED, (e + 1) * LANES)
        shifted[:, spare, :] = jnp.zeros((2, LANES - USED, PIXELS), jnp.bfloat16)
    total = jnp.zeros((128, 2 * LANES), jnp.float32)
    for h in range(2):
        for part in range(2):
            total += lax.dot_general(
                img_ref[:, h, part, :, :HALF].reshape(128, HALF),
                shifted[part, :, h * HALF : (h + 1) * HALF],
                (((1,), (1,)), ((), ())),
                preferred_element_type=jnp.float32,
            )
    pieces = img_ref[:, 0, 0, :, HALF:].reshape(128, LANES).astype(jnp.float32)
    precision = jnp.sum(pieces, axis=1, keepdims=True)
    scaled = precision * (total - jnp.concatenate(halves, axis=1))
    out_ref[...] = scaled.reshape(16, 8, 2 * LANES)


def label_rows(ref0_ref, ref1_ref, straight):
    first = ref0_ref[0].astype(jnp.float32)
    second = ref1_ref[0].astype(jnp.float32)
    low, high = jnp.where(straight, first, second), jnp.where(straight, second, first)
    return jnp.concatenate([as_row(low), as_row(high)], axis=1)


def score_kernel(got_ref, ref0_ref, ref1_ref, prior_ref, zu_ref, score_ref, out_ref):
    labels = label_rows(ref0_ref, ref1_ref, zu_ref[0] == 0)
    prior = jnp.zeros((1, 2 * LANES), jnp.float32)
    for k in range(CLASSES):
        prior = jnp.where(labels == k, prior_ref[k], prior)
    scores = jnp.sum(got_ref[...], axis=0) + prior
    scores = jnp.where(iota((8, 2 * LANES), 1) % LANES < USED, scores, -jnp.inf)
    score_ref[...] = scores
    top = jnp.max(scores, axis=1, keepdims=True)
    weights = jnp.exp(scores - top)
    lane = iota((8, LANES), 1)
    stats = jnp.where(lane == 0, top, 0.0)
    for k in range(CLASSES):
        mass = jnp.sum(jnp.where(labels == k, weights, 0.0), axis=1, keepdims=True)
        stats = jnp.where(lane == k + 1, mass, stats)
    out_ref[...] = jnp.broadcast_to(stats[None], (16, 8, LANES))


def post_kernel(got_ref, score_ref, out_ref):
    got = got_ref[...]
    tops = got[:, :, 0:1]
    top = jnp.max(tops, axis=0)
    lane = iota((8, LANES), 1)
    sums = jnp.sum(got * jnp.exp(tops - top[None]), axis=0)
    sums = jnp.where((lane > 0) & (lane <= CLASSES), sums, 0.0)
    total = jnp.sum(sums, axis=1, keepdims=True)
    classes = pieces_of(sums / total)
    post = jnp.exp(score_ref[...] - top) / total
    mass_row = jnp.sum(post, axis=0, keepdims=True)
    for e in range(2):
        half = slice(e * LANES, (e + 1) * LANES)
        mass = jnp.sum(jnp.where(own_lanes(), mass_row[:, half], 0.0), axis=1, keepdims=True)
        message = jnp.where(lane < USED, post[:, half], 0.0)
        for number, piece in enumerate(pieces_of(mass)):
            message = jnp.where(lane == MASS + number, piece, message)
        if e == 0:
            for number, piece in enumerate(classes):
                message += pltpu.roll(piece, CLASS + CLASSES * number - 1, 1)
        out_ref[:, :, half] = jnp.broadcast_to(message.astype(jnp.bfloat16)[None], (16, 8, LANES))


def back_kernel(got_ref, img_ref, cos_ref, sin_ref, zu_ref, row_ref, out0_ref, out1_ref):
    straight = zu_ref[0] == 0
    got = got_ref[...].astype(jnp.float32)
    extra = jnp.sum(got, axis=0)
    post = got.reshape(128, 2 * LANES)
    post = jnp.where(iota((128, 2 * LANES), 1) % LANES < USED, post, 0.0)
    weights = jnp.transpose(post).astype(jnp.bfloat16)
    for h in range(2):
        cols = slice(h * HALF, (h + 1) * HALF)
        back = [
            jnp.dot(
                weights,
                img_ref[:, h, part, :, :HALF].reshape(128, HALF),
                preferred_element_type=jnp.float32,
            )
            for part in range(2)
        ]
        sums = [jnp.zeros((8, HALF), jnp.float32) for both in range(4)]
        for t in range(SHIFTS):
            cos, sin = cos_ref[t : t + 1, cols], sin_ref[t : t + 1, cols]
            for e in range(2):
                rows = slice(e * LANES + 8 * t, e * LANES + 8 * t + 8)
                back_re, back_im = back[0][rows], back[1][rows]
                sums[2 * e] += back_re * cos - back_im * sin
                sums[2 * e + 1] += back_im * cos + back_re * sin
        for part in range(2):
            low, high = sums[part], sums[2 + part]
            out0_ref[part, :, cols] = jnp.where(straight, low, high)
            out1_ref[part, :, cols] = jnp.where(straight, high, low).astype(jnp.bfloat16)
    lane = iota((8, LANES), 1)
    masses = []
    for e in range(2):
        mine = (lane >= MASS) & (lane < MASS + 3)
        mass = jnp.sum(jnp.where(mine, extra[:, e * LANES : (e + 1) * LANES], 0.0), axis=1, keepdims=True)
        row = jnp.zeros((8, LANES), jnp.float32)
        for number, piece in enumerate(pieces_of(mass)):
            row = jnp.where(lane == MASS + number, piece, row)
        masses.append(row)
    shared = (lane >= CLASS) & (lane < CLASS + 3 * CLASSES)
    for part in range(2):
        classes = got_ref[row_ref[0] + part, :, :LANES].astype(jnp.float32)
        classes = jnp.where(shared, classes, 0.0)
        out0_ref[part, :, PIXELS:] = jnp.where(straight, masses[0], masses[1]) + classes
        out1_ref[part, :, PIXELS:] = (jnp.where(straight, masses[1], masses[0]) + classes).astype(jnp.bfloat16)


def final_kernel(first_ref, second_ref, own_ref, out_ref, class_ref):
    own = own_ref[0] == 1
    lane = iota((8, LANES), 1)
    first, second = first_ref[0, :, PIXELS:], second_ref[0, :, PIXELS:].astype(jnp.float32)
    mine = (lane >= MASS) & (lane < MASS + 3)
    mass = jnp.sum(jnp.where(mine, first + second, 0.0), axis=1, keepdims=True)
    for part in range(2):
        both = first_ref[part, :, :PIXELS] + second_ref[part, :, :PIXELS].astype(jnp.float32)
        out_ref[part] = both / (mass + 1.0)
        classes = jnp.where(own, first_ref[part, :, PIXELS:], second_ref[part, :, PIXELS:].astype(jnp.float32))
        parts = [pltpu.roll(classes, LANES - CLASS - CLASSES * number, 1) for number in range(3)]
        class_ref[8 * part : 8 * part + 8, :] = (parts[0] + parts[1] + parts[2])[:, :CLASSES]


def call(kernel, shapes, args, scratch=(), scalars=0):
    in_vmem = [pl.BlockSpec(memory_space=pltpu.VMEM)] * (len(args) - scalars)
    in_smem = [pl.BlockSpec(memory_space=pltpu.SMEM)] * scalars
    out = [jax.ShapeDtypeStruct(shape, dtype) for shape, dtype in shapes]
    return pl.pallas_call(
        kernel,
        out_shape=out,
        in_specs=in_vmem + in_smem,
        out_specs=[pl.BlockSpec(memory_space=pltpu.VMEM)] * len(out),
        scratch_shapes=list(scratch),
        compiler_params=pltpu.CompilerParams(vmem_limit_bytes=32 << 20),
    )(*args)


def swap(operand, axes):
    return lax.all_to_all(operand, axes, 0, 0, tiled=True)


def local(images, references, precision, shifts, labels, log_prior):
    y, zh, c, zu, zv, xh, xl = (lax.axis_index(name).astype(jnp.int32) for name in ALL)
    half = zu[None]
    (sent,) = call(image_kernel, [((2, 16, HALF + LANES), jnp.bfloat16)], (images, precision[None]))
    sent = lax.ppermute(sent, ALL, IMG_ROUTE)
    units = swap(jnp.broadcast_to(sent[None], (16,) + sent.shape), SPACE).reshape(8, 2, 2, 16, HALF + LANES)
    (low,) = call(ref_kernel, [((2, 8, PIXELS + LANES), jnp.bfloat16)], (references, labels[None]))
    refs = [low, lax.ppermute(low, "zu", SWAP)]
    tags = [ref[:1, :, PIXELS:] for ref in refs]
    cosine, sine = phases(shifts, y * 4 + zh * 2 + c)
    (cross,) = call(
        cross_kernel,
        [((16, 8, 2 * LANES), jnp.float32)],
        (units, *refs, cosine, sine, half),
        [pltpu.VMEM((2, 2 * LANES, PIXELS), jnp.bfloat16)],
        scalars=1,
    )
    scores, stats = call(
        score_kernel,
        [((8, 2 * LANES), jnp.float32), ((16, 8, LANES), jnp.float32)],
        (swap(cross, BLOCK), *tags, log_prior, half),
        scalars=2,
    )
    (post,) = call(post_kernel, [((16, 8, 2 * LANES), jnp.bfloat16)], (swap(stats, SPACE), scores))
    posts = swap(post, BLOCK)
    first, second = call(
        back_kernel,
        [((2, 8, PIXELS + LANES), jnp.float32), ((2, 8, PIXELS + LANES), jnp.bfloat16)],
        (posts, units, cosine, sine, half, 2 * (4 * (y % 2) + 2 * zh + c)[None]),
        scalars=2,
    )
    second = lax.ppermute(second, "zu", SWAP)
    own = (zu == y // 2).astype(jnp.int32)[None]
    return call(
        final_kernel,
        [((2, 8, PIXELS), jnp.float32), ((16, CLASSES), jnp.float32)],
        (first, second, own),
        scalars=1,
    )


def solution(mesh):
    whole = Mesh(mesh.devices.reshape(tuple(SIZES.values())), ALL)
    return jax.shard_map(
        local,
        mesh=whole,
        in_specs=(P(None, IMG, REF), P(None, REF, IMG), P(IMG), P(), P(REF), P()),
        out_specs=(P(None, REF, IMG), P(IMG, None)),
        check_vma=False,
    )
```

```python
import itertools
import math

import jax
import jax.numpy as jnp
from jax import lax
from jax.experimental import pallas as pl
from jax.experimental.pallas import tpu as pltpu
from jax.sharding import Mesh
from jax.sharding import PartitionSpec as P

ROWS = 256
COLS = 128
SHIFTS = 12
CLASSES = 4
LANES = 128
USED = SHIFTS * 8
MASS = USED
CLASS = USED + 4
PIXELS = 2048
HALF = 1024
SIZES = {"y": 4, "zh": 2, "c": 2, "zl": 8, "xh": 2, "xl": 2}
ALL = tuple(SIZES)
IMG = ("y", "zh", "c")
REF = ("zl", "xh", "xl")
SPACE = ("y", "c", "xl")
NEAR = ("y", "xl")
BLOCK = ("zl", "xh")


def place(*coords):
    number = 0
    for size, coord in zip(SIZES.values(), coords, strict=True):
        number = number * size + coord
    return number


def routes(inward):
    made = []
    for r in range(2):
        pairs = []
        for y, zh, c, zl, xh, xl in itertools.product(*(range(size) for size in SIZES.values())):
            work = place(y, zh, c, zl, xh, xl)
            home = place(zl // 2, zl % 2, xh, 2 * y + c, r ^ zh, xl)
            pairs.append((home, work) if inward else (work, home))
        made.append(pairs)
    return made


def phases(shifts, block):
    index = block * PIXELS + jnp.arange(PIXELS, dtype=jnp.int32)
    freq_y = (index // COLS - ROWS // 2).astype(jnp.float32)
    freq_x = (index % COLS).astype(jnp.float32)
    shift_x = shifts[:, 0].astype(jnp.float32)[:, None]
    shift_y = shifts[:, 1].astype(jnp.float32)[:, None]
    angles = 2.0 * math.pi / ROWS * (freq_x[None, :] * shift_x + freq_y[None, :] * shift_y)
    return jnp.cos(angles), jnp.sin(angles)


def iota(shape, axis):
    return lax.broadcasted_iota(jnp.int32, shape, axis)


def own_lanes():
    lane = iota((8, LANES), 1)
    return (lane % 8 == iota((8, LANES), 0)) & (lane < USED)


def as_row(column):
    return jnp.sum(jnp.where(own_lanes(), column, 0.0), axis=0, keepdims=True)


def pieces_of(value):
    first = value.astype(jnp.bfloat16).astype(jnp.float32)
    second = (value - first).astype(jnp.bfloat16).astype(jnp.float32)
    return first, second, value - first - second


def image_kernel(img_ref, precision_ref, out_ref):
    low = img_ref[...].astype(jnp.bfloat16)
    precision = jnp.sum(
        jnp.where(iota((16, 16), 0) == iota((16, 16), 1), precision_ref[...], 0.0), axis=1, keepdims=True
    )
    first, second, third = pieces_of(precision)
    lane = iota((16, LANES), 1)
    pieces = jnp.where(lane == 0, first, jnp.where(lane == 1, second, jnp.where(lane == 2, third, 0.0)))
    pieces = pieces.astype(jnp.bfloat16)
    for copy in range(8):
        out_ref[copy, :, :, :HALF] = low
        out_ref[copy, 0, :, HALF:] = pieces
        out_ref[copy, 1, :, HALF:] = pieces


def ref_kernel(ref_ref, label_ref, out_ref):
    out_ref[:, :, :PIXELS] = ref_ref[...].astype(jnp.bfloat16)
    label = label_ref[...].astype(jnp.float32)
    label = jnp.sum(jnp.where(iota((8, 8), 0) == iota((8, 8), 1), label, 0.0), axis=1, keepdims=True)
    label = jnp.broadcast_to(label, (8, LANES)).astype(jnp.bfloat16)
    out_ref[0, :, PIXELS:] = label
    out_ref[1, :, PIXELS:] = label


def joined(own_ref, other_ref, h, part):
    return jnp.concatenate([ref[:, h, part, :, :HALF].reshape(64, HALF) for ref in (own_ref, other_ref)], axis=0)


def cross_kernel(own_ref, other_ref, ref0_ref, ref1_ref, cos_ref, sin_ref, zh_ref, c_ref, out_ref, shifted):
    straight = zh_ref[0] == 0
    ref0 = ref0_ref[:, :, :PIXELS].astype(jnp.float32)
    ref1 = ref1_ref[:, :, :PIXELS].astype(jnp.float32)
    halves = []
    for e in range(2):
        ref = jnp.where(straight, ref0, ref1) if e == 0 else jnp.where(straight, ref1, ref0)
        re, im = ref[0], ref[1]
        halves.append(as_row(0.5 * jnp.sum(re * re + im * im, axis=1, keepdims=True)))
        for pair in range(SHIFTS // 2):
            rot_re, rot_im = [], []
            for t in (2 * pair, 2 * pair + 1):
                cos, sin = cos_ref[t : t + 1, :], sin_ref[t : t + 1, :]
                rot_re.append(re * cos + im * sin)
                rot_im.append(im * cos - re * sin)
            rows = slice(e * LANES + 16 * pair, e * LANES + 16 * pair + 16)
            shifted[0, rows, :] = jnp.concatenate(rot_re, axis=0).astype(jnp.bfloat16)
            shifted[1, rows, :] = jnp.concatenate(rot_im, axis=0).astype(jnp.bfloat16)
        spare = slice(e * LANES + USED, (e + 1) * LANES)
        shifted[:, spare, :] = jnp.zeros((2, LANES - USED, PIXELS), jnp.bfloat16)
    half = jnp.concatenate(halves, axis=1)
    total = jnp.zeros((128, 2 * LANES), jnp.float32)
    for h in range(2):
        for part in range(2):
            total += lax.dot_general(
                joined(own_ref, other_ref, h, part),
                shifted[part, :, h * HALF : (h + 1) * HALF],
                (((1,), (1,)), ((), ())),
                preferred_element_type=jnp.float32,
            )
    pieces = [ref[:, 0, 0, :, HALF:].reshape(64, LANES).astype(jnp.float32) for ref in (own_ref, other_ref)]
    precision = jnp.sum(jnp.concatenate(pieces, axis=0), axis=1, keepdims=True)
    scaled = (precision * (total - half)).reshape(16, 8, 2 * LANES)
    out_ref[pl.ds(c_ref[0] * 8, 8)] = scaled[:8]
    out_ref[pl.ds((1 - c_ref[0]) * 8, 8)] = scaled[8:]


def label_rows(ref0_ref, ref1_ref, straight):
    first = ref0_ref[0].astype(jnp.float32)
    second = ref1_ref[0].astype(jnp.float32)
    low, high = jnp.where(straight, first, second), jnp.where(straight, second, first)
    return jnp.concatenate([as_row(low), as_row(high)], axis=1)


def score_kernel(got_ref, ref0_ref, ref1_ref, prior_ref, zh_ref, score_ref, out_ref):
    labels = label_rows(ref0_ref, ref1_ref, zh_ref[0] == 0)
    prior = jnp.zeros((1, 2 * LANES), jnp.float32)
    for k in range(CLASSES):
        prior = jnp.where(labels == k, prior_ref[k], prior)
    scores = jnp.sum(got_ref[...], axis=0) + prior
    scores = jnp.where(iota((8, 2 * LANES), 1) % LANES < USED, scores, -jnp.inf)
    score_ref[...] = scores
    top = jnp.max(scores, axis=1, keepdims=True)
    weights = jnp.exp(scores - top)
    lane = iota((8, LANES), 1)
    stats = jnp.where(lane == 0, top, 0.0)
    for k in range(CLASSES):
        mass = jnp.sum(jnp.where(labels == k, weights, 0.0), axis=1, keepdims=True)
        stats = jnp.where(lane == k + 1, mass, stats)
    out_ref[...] = jnp.broadcast_to(stats[None], (16, 8, LANES))


def post_kernel(got_ref, score_ref, out_ref):
    got = got_ref[...]
    tops = got[:, :, 0:1]
    top = jnp.max(tops, axis=0)
    lane = iota((8, LANES), 1)
    sums = jnp.sum(got * jnp.exp(tops - top[None]), axis=0)
    sums = jnp.where((lane > 0) & (lane <= CLASSES), sums, 0.0)
    total = jnp.sum(sums, axis=1, keepdims=True)
    classes = pieces_of(sums / total)
    post = jnp.exp(score_ref[...] - top) / total
    mass_row = jnp.sum(post, axis=0, keepdims=True)
    for e in range(2):
        half = slice(e * LANES, (e + 1) * LANES)
        mass = jnp.sum(jnp.where(own_lanes(), mass_row[:, half], 0.0), axis=1, keepdims=True)
        message = jnp.where(lane < USED, post[:, half], 0.0)
        for number, piece in enumerate(pieces_of(mass)):
            message = jnp.where(lane == MASS + number, piece, message)
        if e == 0:
            for number, piece in enumerate(classes):
                message += pltpu.roll(piece, CLASS + CLASSES * number - 1, 1)
        out_ref[:, :, half] = jnp.broadcast_to(message.astype(jnp.bfloat16)[None], (16, 8, LANES))


def back_kernel(got_ref, own_ref, other_ref, cos_ref, sin_ref, zh_ref, c_ref, out0_ref, out1_ref):
    straight = zh_ref[0] == 0
    extra = jnp.sum(got_ref[...].astype(jnp.float32), axis=0)
    halves = [got_ref[pl.ds(chip * 8, 8)].astype(jnp.float32) for chip in (c_ref[0], 1 - c_ref[0])]
    post = jnp.concatenate(halves, axis=0).reshape(128, 2 * LANES)
    post = jnp.where(iota((128, 2 * LANES), 1) % LANES < USED, post, 0.0)
    weights = jnp.transpose(post).astype(jnp.bfloat16)
    for h in range(2):
        cols = slice(h * HALF, (h + 1) * HALF)
        back = [
            jnp.dot(weights, joined(own_ref, other_ref, h, part), preferred_element_type=jnp.float32)
            for part in range(2)
        ]
        sums = [jnp.zeros((8, HALF), jnp.float32) for both in range(4)]
        for t in range(SHIFTS):
            cos, sin = cos_ref[t : t + 1, cols], sin_ref[t : t + 1, cols]
            for e in range(2):
                rows = slice(e * LANES + 8 * t, e * LANES + 8 * t + 8)
                back_re, back_im = back[0][rows], back[1][rows]
                sums[2 * e] += back_re * cos - back_im * sin
                sums[2 * e + 1] += back_im * cos + back_re * sin
        for part in range(2):
            low, high = sums[part].astype(jnp.bfloat16), sums[2 + part].astype(jnp.bfloat16)
            out0_ref[part, :, cols] = jnp.where(straight, low, high)
            out1_ref[part, :, cols] = jnp.where(straight, high, low)
    lane = iota((8, LANES), 1)
    masses = []
    for e in range(2):
        mine = (lane >= MASS) & (lane < MASS + 3)
        mass = jnp.sum(jnp.where(mine, extra[:, e * LANES : (e + 1) * LANES], 0.0), axis=1, keepdims=True)
        row = jnp.zeros((8, LANES), jnp.float32)
        for number, piece in enumerate(pieces_of(mass)):
            row = jnp.where(lane == number, piece, row)
        masses.append(row.astype(jnp.bfloat16))
    for part in range(2):
        out0_ref[part, :, PIXELS:] = jnp.where(straight, masses[0], masses[1])
        out1_ref[part, :, PIXELS:] = jnp.where(straight, masses[1], masses[0])


def final_kernel(first_ref, second_ref, out_ref):
    extra = first_ref[0, :, PIXELS:].astype(jnp.float32) + second_ref[0, :, PIXELS:].astype(jnp.float32)
    mass = jnp.sum(extra, axis=1, keepdims=True)
    for part in range(2):
        both = first_ref[part, :, :PIXELS].astype(jnp.float32) + second_ref[part, :, :PIXELS].astype(jnp.float32)
        out_ref[part] = both / (mass + 1.0)


def call(kernel, shapes, args, scratch=(), scalars=0, room=32):
    in_vmem = [pl.BlockSpec(memory_space=pltpu.VMEM)] * (len(args) - scalars)
    in_smem = [pl.BlockSpec(memory_space=pltpu.SMEM)] * scalars
    out = [jax.ShapeDtypeStruct(shape, dtype) for shape, dtype in shapes]
    return pl.pallas_call(
        kernel,
        out_shape=out,
        in_specs=in_vmem + in_smem,
        out_specs=[pl.BlockSpec(memory_space=pltpu.VMEM)] * len(out),
        scratch_shapes=list(scratch),
        compiler_params=pltpu.CompilerParams(vmem_limit_bytes=room << 20),
    )(*args)


def swap(operand, axes):
    return lax.all_to_all(operand, axes, 0, 0, tiled=True)


def local(images, references, precision, shifts, labels, log_prior):
    y, zh, c, zl, xh, xl = (lax.axis_index(name) for name in ALL)
    half = zh.astype(jnp.int32)[None]
    (sent,) = call(image_kernel, [((8, 2, 16, HALF + LANES), jnp.bfloat16)], (images, precision[None]), room=60)
    own = swap(sent, NEAR).reshape(4, 2, 2, 16, HALF + LANES)
    other = lax.ppermute(own, "c", [(0, 1), (1, 0)])
    core = c.astype(jnp.int32)[None]
    (low,) = call(ref_kernel, [((2, 8, PIXELS + LANES), jnp.bfloat16)], (references, labels[None]))
    refs = [lax.ppermute(low, ALL, route) for route in routes(True)]
    tags = [ref[:1, :, PIXELS:] for ref in refs]
    cosine, sine = phases(shifts, zl * 2 + xh)
    (cross,) = call(
        cross_kernel,
        [((16, 8, 2 * LANES), jnp.float32)],
        (own, other, *refs, cosine, sine, half, core),
        [pltpu.VMEM((2, 2 * LANES, PIXELS), jnp.bfloat16)],
        scalars=2,
    )
    scores, stats = call(
        score_kernel,
        [((8, 2 * LANES), jnp.float32), ((16, 8, LANES), jnp.float32)],
        (swap(cross, BLOCK), *tags, log_prior, half),
        scalars=2,
    )
    (post,) = call(post_kernel, [((16, 8, 2 * LANES), jnp.bfloat16)], (swap(stats, SPACE), scores))
    posts = swap(post, BLOCK)
    partial = call(
        back_kernel,
        [((2, 8, PIXELS + LANES), jnp.bfloat16)] * 2,
        (posts, own, other, cosine, sine, half, core),
        scalars=2,
    )
    first, second = [lax.ppermute(part, ALL, route) for part, route in zip(partial, routes(False), strict=True)]
    (new_refs,) = call(final_kernel, [((2, 8, PIXELS), jnp.float32)], (first, second))
    mine = lax.dynamic_slice_in_dim(posts, (c * 4 + y) * 2, 2, 0).reshape(16, 2 * LANES)
    shares = mine[:, CLASS : CLASS + 3 * CLASSES].astype(jnp.float32).reshape(16, 3, CLASSES)
    class_post = jnp.sum(shares, axis=1)
    return new_refs, class_post


def solution(mesh):
    whole = Mesh(mesh.devices.reshape(tuple(SIZES.values())), ALL)
    return jax.shard_map(
        local,
        mesh=whole,
        in_specs=(P(None, IMG, REF), P(None, REF, IMG), P(IMG), P(), P(REF), P()),
        out_specs=(P(None, REF, IMG), P(IMG, None)),
        check_vma=False,
    )
```

```python
import itertools
import math

import jax
import jax.numpy as jnp
from jax import lax
from jax.experimental import pallas as pl
from jax.experimental.pallas import tpu as pltpu
from jax.sharding import Mesh
from jax.sharding import PartitionSpec as P

ROWS = 256
COLS = 128
SHIFTS = 12
CLASSES = 4
LANES = 128
USED = SHIFTS * 8
MASS = USED
CLASS = USED + 4
PIXELS = 2048
HALF = 1024
SIZES = {"y": 4, "zh": 2, "c": 2, "zl": 8, "xh": 2, "xl": 2}
ALL = tuple(SIZES)
IMG = ("y", "zh", "c")
REF = ("zl", "xh", "xl")
SPACE = ("y", "xh", "xl")
SWAP = [(0, 1), (1, 0)]
BLOCK = ("zl", "c")


def place(*coords):
    number = 0
    for size, coord in zip(SIZES.values(), coords, strict=True):
        number = number * size + coord
    return number


def routes(inward):
    made = []
    for r in range(2):
        pairs = []
        for y, zh, c, zl, xh, xl in itertools.product(*(range(size) for size in SIZES.values())):
            work = place(y, zh, c, zl, xh, xl)
            home = place(zl // 2, zl % 2, c, 2 * y + (r ^ zh), xh, xl)
            pairs.append((home, work) if inward else (work, home))
        made.append(pairs)
    return made


def phases(shifts, block):
    index = block * PIXELS + jnp.arange(PIXELS, dtype=jnp.int32)
    freq_y = (index // COLS - ROWS // 2).astype(jnp.float32)
    freq_x = (index % COLS).astype(jnp.float32)
    shift_x = shifts[:, 0].astype(jnp.float32)[:, None]
    shift_y = shifts[:, 1].astype(jnp.float32)[:, None]
    angles = 2.0 * math.pi / ROWS * (freq_x[None, :] * shift_x + freq_y[None, :] * shift_y)
    return jnp.cos(angles), jnp.sin(angles)


def iota(shape, axis):
    return lax.broadcasted_iota(jnp.int32, shape, axis)


def own_lanes():
    lane = iota((8, LANES), 1)
    return (lane % 8 == iota((8, LANES), 0)) & (lane < USED)


def as_row(column):
    return jnp.sum(jnp.where(own_lanes(), column, 0.0), axis=0, keepdims=True)


def pieces_of(value):
    first = value.astype(jnp.bfloat16).astype(jnp.float32)
    second = (value - first).astype(jnp.bfloat16).astype(jnp.float32)
    return first, second, value - first - second


def image_kernel(img_ref, precision_ref, out_ref):
    low = img_ref[...].astype(jnp.bfloat16)
    precision = jnp.sum(
        jnp.where(iota((16, 16), 0) == iota((16, 16), 1), precision_ref[...], 0.0), axis=1, keepdims=True
    )
    first, second, third = pieces_of(precision)
    lane = iota((16, LANES), 1)
    pieces = jnp.where(lane == 0, first, jnp.where(lane == 1, second, jnp.where(lane == 2, third, 0.0)))
    pieces = pieces.astype(jnp.bfloat16)
    for copy in range(16):
        out_ref[copy, :, :, :HALF] = low
        out_ref[copy, 0, :, HALF:] = pieces
        out_ref[copy, 1, :, HALF:] = pieces


def ref_kernel(ref_ref, label_ref, out_ref):
    out_ref[:, :, :PIXELS] = ref_ref[...].astype(jnp.bfloat16)
    label = label_ref[...].astype(jnp.float32)
    label = jnp.sum(jnp.where(iota((8, 8), 0) == iota((8, 8), 1), label, 0.0), axis=1, keepdims=True)
    label = jnp.broadcast_to(label, (8, LANES)).astype(jnp.bfloat16)
    out_ref[0, :, PIXELS:] = label
    out_ref[1, :, PIXELS:] = label


def joined(own_ref, other_ref, h, part):
    return jnp.concatenate([ref[:, h, part, :, :HALF].reshape(64, HALF) for ref in (own_ref, other_ref)], axis=0)


def cross_kernel(own_ref, other_ref, ref0_ref, ref1_ref, cos_ref, sin_ref, zh_ref, c_ref, out_ref, shifted):
    straight = zh_ref[0] == 0
    ref0 = ref0_ref[:, :, :PIXELS].astype(jnp.float32)
    ref1 = ref1_ref[:, :, :PIXELS].astype(jnp.float32)
    halves = []
    for e in range(2):
        ref = jnp.where(straight, ref0, ref1) if e == 0 else jnp.where(straight, ref1, ref0)
        re, im = ref[0], ref[1]
        halves.append(as_row(0.5 * jnp.sum(re * re + im * im, axis=1, keepdims=True)))
        for pair in range(SHIFTS // 2):
            rot_re, rot_im = [], []
            for t in (2 * pair, 2 * pair + 1):
                cos, sin = cos_ref[t : t + 1, :], sin_ref[t : t + 1, :]
                rot_re.append(re * cos + im * sin)
                rot_im.append(im * cos - re * sin)
            rows = slice(e * LANES + 16 * pair, e * LANES + 16 * pair + 16)
            shifted[0, rows, :] = jnp.concatenate(rot_re, axis=0).astype(jnp.bfloat16)
            shifted[1, rows, :] = jnp.concatenate(rot_im, axis=0).astype(jnp.bfloat16)
        spare = slice(e * LANES + USED, (e + 1) * LANES)
        shifted[:, spare, :] = jnp.zeros((2, LANES - USED, PIXELS), jnp.bfloat16)
    half = jnp.concatenate(halves, axis=1)
    total = jnp.zeros((128, 2 * LANES), jnp.float32)
    for h in range(2):
        for part in range(2):
            total += lax.dot_general(
                joined(own_ref, other_ref, h, part),
                shifted[part, :, h * HALF : (h + 1) * HALF],
                (((1,), (1,)), ((), ())),
                preferred_element_type=jnp.float32,
            )
    pieces = [ref[:, 0, 0, :, HALF:].reshape(64, LANES).astype(jnp.float32) for ref in (own_ref, other_ref)]
    precision = jnp.sum(jnp.concatenate(pieces, axis=0), axis=1, keepdims=True)
    scaled = (precision * (total - half)).reshape(16, 8, 2 * LANES)
    out_ref[pl.ds(c_ref[0] * 8, 8)] = scaled[:8]
    out_ref[pl.ds((1 - c_ref[0]) * 8, 8)] = scaled[8:]


def label_rows(ref0_ref, ref1_ref, straight):
    first = ref0_ref[0].astype(jnp.float32)
    second = ref1_ref[0].astype(jnp.float32)
    low, high = jnp.where(straight, first, second), jnp.where(straight, second, first)
    return jnp.concatenate([as_row(low), as_row(high)], axis=1)


def score_kernel(got_ref, ref0_ref, ref1_ref, prior_ref, zh_ref, score_ref, out_ref):
    labels = label_rows(ref0_ref, ref1_ref, zh_ref[0] == 0)
    prior = jnp.zeros((1, 2 * LANES), jnp.float32)
    for k in range(CLASSES):
        prior = jnp.where(labels == k, prior_ref[k], prior)
    scores = jnp.sum(got_ref[...], axis=0) + prior
    scores = jnp.where(iota((8, 2 * LANES), 1) % LANES < USED, scores, -jnp.inf)
    score_ref[...] = scores
    top = jnp.max(scores, axis=1, keepdims=True)
    weights = jnp.exp(scores - top)
    lane = iota((8, LANES), 1)
    stats = jnp.where(lane == 0, top, 0.0)
    for k in range(CLASSES):
        mass = jnp.sum(jnp.where(labels == k, weights, 0.0), axis=1, keepdims=True)
        stats = jnp.where(lane == k + 1, mass, stats)
    out_ref[...] = jnp.broadcast_to(stats[None], (16, 8, LANES))


def post_kernel(got_ref, score_ref, out_ref):
    got = got_ref[...]
    tops = got[:, :, 0:1]
    top = jnp.max(tops, axis=0)
    lane = iota((8, LANES), 1)
    sums = jnp.sum(got * jnp.exp(tops - top[None]), axis=0)
    sums = jnp.where((lane > 0) & (lane <= CLASSES), sums, 0.0)
    total = jnp.sum(sums, axis=1, keepdims=True)
    classes = pieces_of(sums / total)
    post = jnp.exp(score_ref[...] - top) / total
    mass_row = jnp.sum(post, axis=0, keepdims=True)
    for e in range(2):
        half = slice(e * LANES, (e + 1) * LANES)
        mass = jnp.sum(jnp.where(own_lanes(), mass_row[:, half], 0.0), axis=1, keepdims=True)
        message = jnp.where(lane < USED, post[:, half], 0.0)
        for number, piece in enumerate(pieces_of(mass)):
            message = jnp.where(lane == MASS + number, piece, message)
        if e == 0:
            for number, piece in enumerate(classes):
                message += pltpu.roll(piece, CLASS + CLASSES * number - 1, 1)
        out_ref[:, :, half] = jnp.broadcast_to(message.astype(jnp.bfloat16)[None], (16, 8, LANES))


def back_kernel(got_ref, own_ref, other_ref, cos_ref, sin_ref, zh_ref, c_ref, out0_ref, out1_ref):
    straight = zh_ref[0] == 0
    extra = jnp.sum(got_ref[...].astype(jnp.float32), axis=0)
    halves = [got_ref[pl.ds(chip * 8, 8)].astype(jnp.float32) for chip in (c_ref[0], 1 - c_ref[0])]
    post = jnp.concatenate(halves, axis=0).reshape(128, 2 * LANES)
    post = jnp.where(iota((128, 2 * LANES), 1) % LANES < USED, post, 0.0)
    weights = jnp.transpose(post).astype(jnp.bfloat16)
    for h in range(2):
        cols = slice(h * HALF, (h + 1) * HALF)
        back = [
            jnp.dot(weights, joined(own_ref, other_ref, h, part), preferred_element_type=jnp.float32)
            for part in range(2)
        ]
        sums = [jnp.zeros((8, HALF), jnp.float32) for both in range(4)]
        for t in range(SHIFTS):
            cos, sin = cos_ref[t : t + 1, cols], sin_ref[t : t + 1, cols]
            for e in range(2):
                rows = slice(e * LANES + 8 * t, e * LANES + 8 * t + 8)
                back_re, back_im = back[0][rows], back[1][rows]
                sums[2 * e] += back_re * cos - back_im * sin
                sums[2 * e + 1] += back_im * cos + back_re * sin
        for part in range(2):
            low, high = sums[part].astype(jnp.bfloat16), sums[2 + part].astype(jnp.bfloat16)
            out0_ref[part, :, cols] = jnp.where(straight, low, high)
            out1_ref[part, :, cols] = jnp.where(straight, high, low)
    lane = iota((8, LANES), 1)
    masses = []
    for e in range(2):
        mine = (lane >= MASS) & (lane < MASS + 3)
        mass = jnp.sum(jnp.where(mine, extra[:, e * LANES : (e + 1) * LANES], 0.0), axis=1, keepdims=True)
        row = jnp.zeros((8, LANES), jnp.float32)
        for number, piece in enumerate(pieces_of(mass)):
            row = jnp.where(lane == number, piece, row)
        masses.append(row.astype(jnp.bfloat16))
    for part in range(2):
        out0_ref[part, :, PIXELS:] = jnp.where(straight, masses[0], masses[1])
        out1_ref[part, :, PIXELS:] = jnp.where(straight, masses[1], masses[0])


def final_kernel(first_ref, second_ref, out_ref):
    extra = first_ref[0, :, PIXELS:].astype(jnp.float32) + second_ref[0, :, PIXELS:].astype(jnp.float32)
    mass = jnp.sum(extra, axis=1, keepdims=True)
    for part in range(2):
        both = first_ref[part, :, :PIXELS].astype(jnp.float32) + second_ref[part, :, :PIXELS].astype(jnp.float32)
        out_ref[part] = both / (mass + 1.0)


def call(kernel, shapes, args, scratch=(), scalars=0, room=32):
    in_vmem = [pl.BlockSpec(memory_space=pltpu.VMEM)] * (len(args) - scalars)
    in_smem = [pl.BlockSpec(memory_space=pltpu.SMEM)] * scalars
    out = [jax.ShapeDtypeStruct(shape, dtype) for shape, dtype in shapes]
    return pl.pallas_call(
        kernel,
        out_shape=out,
        in_specs=in_vmem + in_smem,
        out_specs=[pl.BlockSpec(memory_space=pltpu.VMEM)] * len(out),
        scratch_shapes=list(scratch),
        compiler_params=pltpu.CompilerParams(vmem_limit_bytes=room << 20),
    )(*args)


def swap(operand, axes):
    return lax.all_to_all(operand, axes, 0, 0, tiled=True)


def local(images, references, precision, shifts, labels, log_prior):
    y, zh, c, zl, xh, xl = (lax.axis_index(name) for name in ALL)
    half = zh.astype(jnp.int32)[None]
    (sent,) = call(image_kernel, [((16, 2, 16, HALF + LANES), jnp.bfloat16)], (images, precision[None]), room=60)
    units = swap(sent, SPACE).reshape(4, 2, 2, 2, 16, HALF + LANES)
    own = lax.dynamic_index_in_dim(units, c, 1, keepdims=False)
    other = lax.dynamic_index_in_dim(units, 1 - c, 1, keepdims=False)
    other = lax.ppermute(other, "c", SWAP)
    core = c.astype(jnp.int32)[None]
    (low,) = call(ref_kernel, [((2, 8, PIXELS + LANES), jnp.bfloat16)], (references, labels[None]))
    refs = [lax.ppermute(low, ALL, route) for route in routes(True)]
    tags = [ref[:1, :, PIXELS:] for ref in refs]
    cosine, sine = phases(shifts, zl * 2 + c)
    (cross,) = call(
        cross_kernel,
        [((16, 8, 2 * LANES), jnp.float32)],
        (own, other, *refs, cosine, sine, half, core),
        [pltpu.VMEM((2, 2 * LANES, PIXELS), jnp.bfloat16)],
        scalars=2,
    )
    scores, stats = call(
        score_kernel,
        [((8, 2 * LANES), jnp.float32), ((16, 8, LANES), jnp.float32)],
        (swap(cross, BLOCK), *tags, log_prior, half),
        scalars=2,
    )
    (post,) = call(post_kernel, [((16, 8, 2 * LANES), jnp.bfloat16)], (swap(stats, SPACE), scores))
    posts = swap(post, BLOCK)
    partial = call(
        back_kernel,
        [((2, 8, PIXELS + LANES), jnp.bfloat16)] * 2,
        (posts, own, other, cosine, sine, half, core),
        scalars=2,
    )
    first, second = [lax.ppermute(part, ALL, route) for part, route in zip(partial, routes(False), strict=True)]
    (new_refs,) = call(final_kernel, [((2, 8, PIXELS), jnp.float32)], (first, second))
    mine = lax.dynamic_slice_in_dim(posts, (c * 4 + y) * 2, 2, 0).reshape(16, 2 * LANES)
    shares = mine[:, CLASS : CLASS + 3 * CLASSES].astype(jnp.float32).reshape(16, 3, CLASSES)
    class_post = jnp.sum(shares, axis=1)
    return new_refs, class_post


def solution(mesh):
    whole = Mesh(mesh.devices.reshape(tuple(SIZES.values())), ALL)
    return jax.shard_map(
        local,
        mesh=whole,
        in_specs=(P(None, IMG, REF), P(None, REF, IMG), P(IMG), P(), P(REF), P()),
        out_specs=(P(None, REF, IMG), P(IMG, None)),
        check_vma=False,
    )
```

```python
import itertools
import math

import jax
import jax.numpy as jnp
from jax import lax
from jax.experimental import pallas as pl
from jax.experimental.pallas import tpu as pltpu
from jax.sharding import Mesh
from jax.sharding import PartitionSpec as P

ROWS = 256
COLS = 128
SHIFTS = 12
CLASSES = 4
LANES = 128
USED = SHIFTS * 8
MASS = USED
CLASS = USED + 4
PIXELS = 2048
HALF = 1024
SIZES = {"y": 4, "zh": 2, "c": 2, "zl": 8, "xh": 2, "xl": 2}
ALL = tuple(SIZES)
IMG = ("y", "zh", "c")
REF = ("zl", "xh", "xl")
SPACE = ("y", "xh", "xl")
SWAP = [(0, 1), (1, 0)]
BLOCK = ("zl", "c")


def place(*coords):
    number = 0
    for size, coord in zip(SIZES.values(), coords, strict=True):
        number = number * size + coord
    return number


def routes(inward):
    made = []
    for r in range(2):
        pairs = []
        for y, zh, c, zl, xh, xl in itertools.product(*(range(size) for size in SIZES.values())):
            work = place(y, zh, c, zl, xh, xl)
            home = place(zl // 2, zl % 2, c, 2 * y + (r ^ zh), xh, xl)
            pairs.append((home, work) if inward else (work, home))
        made.append(pairs)
    return made


def phases(shifts, block):
    index = block * PIXELS + jnp.arange(PIXELS, dtype=jnp.int32)
    freq_y = (index // COLS - ROWS // 2).astype(jnp.float32)
    freq_x = (index % COLS).astype(jnp.float32)
    shift_x = shifts[:, 0].astype(jnp.float32)[:, None]
    shift_y = shifts[:, 1].astype(jnp.float32)[:, None]
    angles = 2.0 * math.pi / ROWS * (freq_x[None, :] * shift_x + freq_y[None, :] * shift_y)
    return jnp.cos(angles), jnp.sin(angles)


def iota(shape, axis):
    return lax.broadcasted_iota(jnp.int32, shape, axis)


def own_lanes():
    lane = iota((8, LANES), 1)
    return (lane % 8 == iota((8, LANES), 0)) & (lane < USED)


def as_row(column):
    return jnp.sum(jnp.where(own_lanes(), column, 0.0), axis=0, keepdims=True)


def pieces_of(value):
    first = value.astype(jnp.bfloat16).astype(jnp.float32)
    second = (value - first).astype(jnp.bfloat16).astype(jnp.float32)
    return first, second, value - first - second


def image_kernel(img_ref, precision_ref, out_ref):
    low = img_ref[...].astype(jnp.bfloat16)
    precision = jnp.sum(
        jnp.where(iota((16, 16), 0) == iota((16, 16), 1), precision_ref[...], 0.0), axis=1, keepdims=True
    )
    first, second, third = pieces_of(precision)
    lane = iota((16, LANES), 1)
    pieces = jnp.where(lane == 0, first, jnp.where(lane == 1, second, jnp.where(lane == 2, third, 0.0)))
    pieces = pieces.astype(jnp.bfloat16)
    for copy in range(16):
        out_ref[copy, :, :, :HALF] = low
        out_ref[copy, 0, :, HALF:] = pieces
        out_ref[copy, 1, :, HALF:] = pieces


def ref_kernel(ref_ref, label_ref, out_ref):
    out_ref[:, :, :PIXELS] = ref_ref[...].astype(jnp.bfloat16)
    label = label_ref[...].astype(jnp.float32)
    label = jnp.sum(jnp.where(iota((8, 8), 0) == iota((8, 8), 1), label, 0.0), axis=1, keepdims=True)
    label = jnp.broadcast_to(label, (8, LANES)).astype(jnp.bfloat16)
    out_ref[0, :, PIXELS:] = label
    out_ref[1, :, PIXELS:] = label


def joined(own_ref, other_ref, h, part):
    return jnp.concatenate([ref[:, h, part, :, :HALF].reshape(64, HALF) for ref in (own_ref, other_ref)], axis=0)


def rotate_kernel(ref_ref, cos_ref, sin_ref, shifted, row_ref):
    re = ref_ref[0, :, :PIXELS].astype(jnp.float32)
    im = ref_ref[1, :, :PIXELS].astype(jnp.float32)
    row_ref[0:1, :] = as_row(0.5 * jnp.sum(re * re + im * im, axis=1, keepdims=True))
    row_ref[1:2, :] = as_row(ref_ref[0, :, PIXELS:].astype(jnp.float32))
    for pair in range(SHIFTS // 2):
        rot_re, rot_im = [], []
        for t in (2 * pair, 2 * pair + 1):
            cos, sin = cos_ref[t : t + 1, :], sin_ref[t : t + 1, :]
            rot_re.append(re * cos + im * sin)
            rot_im.append(im * cos - re * sin)
        rows = slice(16 * pair, 16 * pair + 16)
        shifted[0, rows, :] = jnp.concatenate(rot_re, axis=0).astype(jnp.bfloat16)
        shifted[1, rows, :] = jnp.concatenate(rot_im, axis=0).astype(jnp.bfloat16)
    shifted[:, USED:, :] = jnp.zeros((2, LANES - USED, PIXELS), jnp.bfloat16)


def cross_kernel(own_ref, other_ref, first_ref, second_ref, row0_ref, row1_ref, zh_ref, c_ref, out_ref):
    total = jnp.zeros((128, 2 * LANES), jnp.float32)
    for h in range(2):
        cols = slice(h * HALF, (h + 1) * HALF)
        for part in range(2):
            total += lax.dot_general(
                joined(own_ref, other_ref, h, part),
                jnp.concatenate([first_ref[part, :, cols], second_ref[part, :, cols]], axis=0),
                (((1,), (1,)), ((), ())),
                preferred_element_type=jnp.float32,
            )
    total -= jnp.concatenate([row0_ref[0:1, :], row1_ref[0:1, :]], axis=1)
    pieces = [ref[:, 0, 0, :, HALF:].reshape(64, LANES).astype(jnp.float32) for ref in (own_ref, other_ref)]
    precision = jnp.sum(jnp.concatenate(pieces, axis=0), axis=1, keepdims=True)
    scaled = precision * total
    straight = zh_ref[0] == 0
    left, right = scaled[:, :LANES], scaled[:, LANES:]
    sides = [jnp.where(straight, left, right), jnp.where(straight, right, left)]
    for e in range(2):
        side = sides[e].reshape(16, 8, LANES)
        lanes = slice(e * LANES, (e + 1) * LANES)
        out_ref[pl.ds(c_ref[0] * 8, 8), :, lanes] = side[:8]
        out_ref[pl.ds((1 - c_ref[0]) * 8, 8), :, lanes] = side[8:]


def score_kernel(got_ref, row0_ref, row1_ref, prior_ref, zh_ref, score_ref, out_ref):
    straight = zh_ref[0] == 0
    first, second = row0_ref[1:2, :], row1_ref[1:2, :]
    labels = jnp.concatenate([jnp.where(straight, first, second), jnp.where(straight, second, first)], axis=1)
    prior = jnp.zeros((1, 2 * LANES), jnp.float32)
    for k in range(CLASSES):
        prior = jnp.where(labels == k, prior_ref[k], prior)
    scores = jnp.sum(got_ref[...], axis=0) + prior
    scores = jnp.where(iota((8, 2 * LANES), 1) % LANES < USED, scores, -jnp.inf)
    score_ref[...] = scores
    top = jnp.max(scores, axis=1, keepdims=True)
    weights = jnp.exp(scores - top)
    lane = iota((8, LANES), 1)
    stats = jnp.where(lane == 0, top, 0.0)
    for k in range(CLASSES):
        mass = jnp.sum(jnp.where(labels == k, weights, 0.0), axis=1, keepdims=True)
        stats = jnp.where(lane == k + 1, mass, stats)
    out_ref[...] = jnp.broadcast_to(stats[None], (16, 8, LANES))


def post_kernel(got_ref, score_ref, out_ref):
    got = got_ref[...]
    tops = got[:, :, 0:1]
    top = jnp.max(tops, axis=0)
    lane = iota((8, LANES), 1)
    sums = jnp.sum(got * jnp.exp(tops - top[None]), axis=0)
    sums = jnp.where((lane > 0) & (lane <= CLASSES), sums, 0.0)
    total = jnp.sum(sums, axis=1, keepdims=True)
    classes = pieces_of(sums / total)
    post = jnp.exp(score_ref[...] - top) / total
    mass_row = jnp.sum(post, axis=0, keepdims=True)
    for e in range(2):
        half = slice(e * LANES, (e + 1) * LANES)
        mass = jnp.sum(jnp.where(own_lanes(), mass_row[:, half], 0.0), axis=1, keepdims=True)
        message = jnp.where(lane < USED, post[:, half], 0.0)
        for number, piece in enumerate(pieces_of(mass)):
            message = jnp.where(lane == MASS + number, piece, message)
        if e == 0:
            for number, piece in enumerate(classes):
                message += pltpu.roll(piece, CLASS + CLASSES * number - 1, 1)
        out_ref[:, :, half] = jnp.broadcast_to(message.astype(jnp.bfloat16)[None], (16, 8, LANES))


def back_kernel(got_ref, own_ref, other_ref, cos_ref, sin_ref, zh_ref, c_ref, out0_ref, out1_ref):
    straight = zh_ref[0] == 0
    extra = jnp.sum(got_ref[...].astype(jnp.float32), axis=0)
    halves = [got_ref[pl.ds(chip * 8, 8)].astype(jnp.float32) for chip in (c_ref[0], 1 - c_ref[0])]
    post = jnp.concatenate(halves, axis=0).reshape(128, 2 * LANES)
    post = jnp.where(iota((128, 2 * LANES), 1) % LANES < USED, post, 0.0)
    weights = jnp.transpose(post).astype(jnp.bfloat16)
    for h in range(2):
        cols = slice(h * HALF, (h + 1) * HALF)
        back = [
            jnp.dot(weights, joined(own_ref, other_ref, h, part), preferred_element_type=jnp.float32)
            for part in range(2)
        ]
        sums = [jnp.zeros((8, HALF), jnp.float32) for both in range(4)]
        for t in range(SHIFTS):
            cos, sin = cos_ref[t : t + 1, cols], sin_ref[t : t + 1, cols]
            for e in range(2):
                rows = slice(e * LANES + 8 * t, e * LANES + 8 * t + 8)
                back_re, back_im = back[0][rows], back[1][rows]
                sums[2 * e] += back_re * cos - back_im * sin
                sums[2 * e + 1] += back_im * cos + back_re * sin
        for part in range(2):
            low, high = sums[part].astype(jnp.bfloat16), sums[2 + part].astype(jnp.bfloat16)
            out0_ref[part, :, cols] = jnp.where(straight, low, high)
            out1_ref[part, :, cols] = jnp.where(straight, high, low)
    lane = iota((8, LANES), 1)
    masses = []
    for e in range(2):
        mine = (lane >= MASS) & (lane < MASS + 3)
        mass = jnp.sum(jnp.where(mine, extra[:, e * LANES : (e + 1) * LANES], 0.0), axis=1, keepdims=True)
        row = jnp.zeros((8, LANES), jnp.float32)
        for number, piece in enumerate(pieces_of(mass)):
            row = jnp.where(lane == number, piece, row)
        masses.append(row.astype(jnp.bfloat16))
    for part in range(2):
        out0_ref[part, :, PIXELS:] = jnp.where(straight, masses[0], masses[1])
        out1_ref[part, :, PIXELS:] = jnp.where(straight, masses[1], masses[0])


def final_kernel(first_ref, second_ref, out_ref):
    extra = first_ref[0, :, PIXELS:].astype(jnp.float32) + second_ref[0, :, PIXELS:].astype(jnp.float32)
    mass = jnp.sum(extra, axis=1, keepdims=True)
    for part in range(2):
        both = first_ref[part, :, :PIXELS].astype(jnp.float32) + second_ref[part, :, :PIXELS].astype(jnp.float32)
        out_ref[part] = both / (mass + 1.0)


def call(kernel, shapes, args, scratch=(), scalars=0, room=12):
    in_vmem = [pl.BlockSpec(memory_space=pltpu.VMEM)] * (len(args) - scalars)
    in_smem = [pl.BlockSpec(memory_space=pltpu.SMEM)] * scalars
    out = [jax.ShapeDtypeStruct(shape, dtype) for shape, dtype in shapes]
    return pl.pallas_call(
        kernel,
        out_shape=out,
        in_specs=in_vmem + in_smem,
        out_specs=[pl.BlockSpec(memory_space=pltpu.VMEM)] * len(out),
        scratch_shapes=list(scratch),
        compiler_params=pltpu.CompilerParams(vmem_limit_bytes=room << 20),
    )(*args)


def swap(operand, axes):
    return lax.all_to_all(operand, axes, 0, 0, tiled=True)


def local(images, references, precision, shifts, labels, log_prior):
    y, zh, c, zl, xh, xl = (lax.axis_index(name) for name in ALL)
    half = zh.astype(jnp.int32)[None]
    (sent,) = call(image_kernel, [((16, 2, 16, HALF + LANES), jnp.bfloat16)], (images, precision[None]), room=60)
    units = swap(sent, SPACE).reshape(4, 2, 2, 2, 16, HALF + LANES)
    own = lax.dynamic_index_in_dim(units, c, 1, keepdims=False)
    other = lax.dynamic_index_in_dim(units, 1 - c, 1, keepdims=False)
    other = lax.ppermute(other, "c", SWAP)
    core = c.astype(jnp.int32)[None]
    (low,) = call(ref_kernel, [((2, 8, PIXELS + LANES), jnp.bfloat16)], (references, labels[None]))
    refs = [lax.ppermute(low, ALL, route) for route in routes(True)]
    cosine, sine = phases(shifts, zl * 2 + c)
    rotated = [
        call(
            rotate_kernel,
            [((2, LANES, PIXELS), jnp.bfloat16), ((2, LANES), jnp.float32)],
            (ref, cosine, sine),
            room=8,
        )
        for ref in refs
    ]
    (first, row0), (second, row1) = rotated
    (cross,) = call(
        cross_kernel,
        [((16, 8, 2 * LANES), jnp.float32)],
        (own, other, first, second, row0, row1, half, core),
        scalars=2,
        room=16,
    )
    scores, stats = call(
        score_kernel,
        [((8, 2 * LANES), jnp.float32), ((16, 8, LANES), jnp.float32)],
        (swap(cross, BLOCK), row0, row1, log_prior, half),
        scalars=2,
    )
    (post,) = call(post_kernel, [((16, 8, 2 * LANES), jnp.bfloat16)], (swap(stats, SPACE), scores))
    posts = swap(post, BLOCK)
    partial = call(
        back_kernel,
        [((2, 8, PIXELS + LANES), jnp.bfloat16)] * 2,
        (posts, own, other, cosine, sine, half, core),
        scalars=2,
    )
    first, second = [lax.ppermute(part, ALL, route) for part, route in zip(partial, routes(False), strict=True)]
    (new_refs,) = call(final_kernel, [((2, 8, PIXELS), jnp.float32)], (first, second))
    mine = lax.dynamic_slice_in_dim(posts, (c * 4 + y) * 2, 2, 0).reshape(16, 2 * LANES)
    shares = mine[:, CLASS : CLASS + 3 * CLASSES].astype(jnp.float32).reshape(16, 3, CLASSES)
    class_post = jnp.sum(shares, axis=1)
    return new_refs, class_post


def solution(mesh):
    whole = Mesh(mesh.devices.reshape(tuple(SIZES.values())), ALL)
    return jax.shard_map(
        local,
        mesh=whole,
        in_specs=(P(None, IMG, REF), P(None, REF, IMG), P(IMG), P(), P(REF), P()),
        out_specs=(P(None, REF, IMG), P(IMG, None)),
        check_vma=False,
    )
```

```python
import itertools
import math

import jax
import jax.numpy as jnp
from jax import lax
from jax.experimental import pallas as pl
from jax.experimental.pallas import tpu as pltpu
from jax.sharding import Mesh
from jax.sharding import PartitionSpec as P

ROWS = 256
COLS = 128
SHIFTS = 12
CLASSES = 4
LANES = 128
USED = SHIFTS * 8
MASS = USED
CLASS = USED + 4
PIXELS = 2048
HALF = 1024
SIZES = {"y": 4, "zh": 2, "c": 2, "zl": 8, "xh": 2, "xl": 2}
ALL = tuple(SIZES)
IMG = ("y", "zh", "c")
REF = ("zl", "xh", "xl")
SPACE = ("y", "xh", "xl")
SWAP = [(0, 1), (1, 0)]
BLOCK = ("zl", "c")


def place(*coords):
    number = 0
    for size, coord in zip(SIZES.values(), coords, strict=True):
        number = number * size + coord
    return number


def routes(inward):
    made = []
    for r in range(2):
        pairs = []
        for y, zh, c, zl, xh, xl in itertools.product(*(range(size) for size in SIZES.values())):
            work = place(y, zh, c, zl, xh, xl)
            home = place(zl // 2, zl % 2, c, 2 * y + (r ^ zh), xh, xl)
            pairs.append((home, work) if inward else (work, home))
        made.append(pairs)
    return made


def phases(shifts, block):
    index = block * PIXELS + jnp.arange(PIXELS, dtype=jnp.int32)
    freq_y = (index // COLS - ROWS // 2).astype(jnp.float32)
    freq_x = (index % COLS).astype(jnp.float32)
    shift_x = shifts[:, 0].astype(jnp.float32)[:, None]
    shift_y = shifts[:, 1].astype(jnp.float32)[:, None]
    angles = 2.0 * math.pi / ROWS * (freq_x[None, :] * shift_x + freq_y[None, :] * shift_y)
    return jnp.cos(angles), jnp.sin(angles)


def iota(shape, axis):
    return lax.broadcasted_iota(jnp.int32, shape, axis)


def own_lanes():
    lane = iota((8, LANES), 1)
    return (lane % 8 == iota((8, LANES), 0)) & (lane < USED)


def as_row(column):
    return jnp.sum(jnp.where(own_lanes(), column, 0.0), axis=0, keepdims=True)


def pieces_of(value):
    first = value.astype(jnp.bfloat16).astype(jnp.float32)
    second = (value - first).astype(jnp.bfloat16).astype(jnp.float32)
    return first, second, value - first - second


def image_kernel(img_ref, precision_ref, out_hbm, block, sems):
    low = img_ref[...].astype(jnp.bfloat16)
    precision = jnp.sum(
        jnp.where(iota((16, 16), 0) == iota((16, 16), 1), precision_ref[...], 0.0), axis=1, keepdims=True
    )
    first, second, third = pieces_of(precision)
    lane = iota((16, LANES), 1)
    pieces = jnp.where(lane == 0, first, jnp.where(lane == 1, second, jnp.where(lane == 2, third, 0.0)))
    pieces = pieces.astype(jnp.bfloat16)
    block[:, :, :HALF] = low
    block[0, :, HALF:] = pieces
    block[1, :, HALF:] = pieces
    copies = [pltpu.make_async_copy(block, out_hbm.at[slot], sems.at[slot]) for slot in range(16)]
    for copy in copies:
        copy.start()
    for copy in copies:
        copy.wait()


def ref_kernel(ref_ref, label_ref, out_ref):
    out_ref[:, :, :PIXELS] = ref_ref[...].astype(jnp.bfloat16)
    label = label_ref[...].astype(jnp.float32)
    label = jnp.sum(jnp.where(iota((8, 8), 0) == iota((8, 8), 1), label, 0.0), axis=1, keepdims=True)
    label = jnp.broadcast_to(label, (8, LANES)).astype(jnp.bfloat16)
    out_ref[0, :, PIXELS:] = label
    out_ref[1, :, PIXELS:] = label


def joined(own_ref, other_ref, h, part):
    return jnp.concatenate([ref[:, h, part, :, :HALF].reshape(64, HALF) for ref in (own_ref, other_ref)], axis=0)


def rotate_kernel(ref_ref, cos_ref, sin_ref, shifted, row_ref):
    re = ref_ref[0, :, :PIXELS].astype(jnp.float32)
    im = ref_ref[1, :, :PIXELS].astype(jnp.float32)
    row_ref[0:1, :] = as_row(0.5 * jnp.sum(re * re + im * im, axis=1, keepdims=True))
    row_ref[1:2, :] = as_row(ref_ref[0, :, PIXELS:].astype(jnp.float32))
    for pair in range(SHIFTS // 2):
        rot_re, rot_im = [], []
        for t in (2 * pair, 2 * pair + 1):
            cos, sin = cos_ref[t : t + 1, :], sin_ref[t : t + 1, :]
            rot_re.append(re * cos + im * sin)
            rot_im.append(im * cos - re * sin)
        rows = slice(16 * pair, 16 * pair + 16)
        shifted[0, rows, :] = jnp.concatenate(rot_re, axis=0).astype(jnp.bfloat16)
        shifted[1, rows, :] = jnp.concatenate(rot_im, axis=0).astype(jnp.bfloat16)
    shifted[:, USED:, :] = jnp.zeros((2, LANES - USED, PIXELS), jnp.bfloat16)


def cross_kernel(own_ref, other_ref, first_ref, second_ref, row0_ref, row1_ref, zh_ref, c_ref, out_ref):
    total = jnp.zeros((128, 2 * LANES), jnp.float32)
    for h in range(2):
        cols = slice(h * HALF, (h + 1) * HALF)
        for part in range(2):
            total += lax.dot_general(
                joined(own_ref, other_ref, h, part),
                jnp.concatenate([first_ref[part, :, cols], second_ref[part, :, cols]], axis=0),
                (((1,), (1,)), ((), ())),
                preferred_element_type=jnp.float32,
            )
    total -= jnp.concatenate([row0_ref[0:1, :], row1_ref[0:1, :]], axis=1)
    pieces = [ref[:, 0, 0, :, HALF:].reshape(64, LANES).astype(jnp.float32) for ref in (own_ref, other_ref)]
    precision = jnp.sum(jnp.concatenate(pieces, axis=0), axis=1, keepdims=True)
    scaled = precision * total
    straight = zh_ref[0] == 0
    left, right = scaled[:, :LANES], scaled[:, LANES:]
    sides = [jnp.where(straight, left, right), jnp.where(straight, right, left)]
    for e in range(2):
        side = sides[e].reshape(16, 8, LANES)
        lanes = slice(e * LANES, (e + 1) * LANES)
        out_ref[pl.ds(c_ref[0] * 8, 8), :, lanes] = side[:8]
        out_ref[pl.ds((1 - c_ref[0]) * 8, 8), :, lanes] = side[8:]


def score_kernel(got_ref, row0_ref, row1_ref, prior_ref, zh_ref, score_ref, out_ref):
    straight = zh_ref[0] == 0
    first, second = row0_ref[1:2, :], row1_ref[1:2, :]
    labels = jnp.concatenate([jnp.where(straight, first, second), jnp.where(straight, second, first)], axis=1)
    prior = jnp.zeros((1, 2 * LANES), jnp.float32)
    for k in range(CLASSES):
        prior = jnp.where(labels == k, prior_ref[k], prior)
    scores = jnp.sum(got_ref[...], axis=0) + prior
    scores = jnp.where(iota((8, 2 * LANES), 1) % LANES < USED, scores, -jnp.inf)
    score_ref[...] = scores
    top = jnp.max(scores, axis=1, keepdims=True)
    weights = jnp.exp(scores - top)
    lane = iota((8, LANES), 1)
    stats = jnp.where(lane == 0, top, 0.0)
    for k in range(CLASSES):
        mass = jnp.sum(jnp.where(labels == k, weights, 0.0), axis=1, keepdims=True)
        stats = jnp.where(lane == k + 1, mass, stats)
    out_ref[...] = jnp.broadcast_to(stats[None], (16, 8, LANES))


def post_kernel(got_ref, score_ref, out_ref):
    got = got_ref[...]
    tops = got[:, :, 0:1]
    top = jnp.max(tops, axis=0)
    lane = iota((8, LANES), 1)
    sums = jnp.sum(got * jnp.exp(tops - top[None]), axis=0)
    sums = jnp.where((lane > 0) & (lane <= CLASSES), sums, 0.0)
    total = jnp.sum(sums, axis=1, keepdims=True)
    classes = pieces_of(sums / total)
    post = jnp.exp(score_ref[...] - top) / total
    mass_row = jnp.sum(post, axis=0, keepdims=True)
    for e in range(2):
        half = slice(e * LANES, (e + 1) * LANES)
        mass = jnp.sum(jnp.where(own_lanes(), mass_row[:, half], 0.0), axis=1, keepdims=True)
        message = jnp.where(lane < USED, post[:, half], 0.0)
        for number, piece in enumerate(pieces_of(mass)):
            message = jnp.where(lane == MASS + number, piece, message)
        if e == 0:
            for number, piece in enumerate(classes):
                message += pltpu.roll(piece, CLASS + CLASSES * number - 1, 1)
        out_ref[:, :, half] = jnp.broadcast_to(message.astype(jnp.bfloat16)[None], (16, 8, LANES))


def back_kernel(got_ref, own_ref, other_ref, cos_ref, sin_ref, zh_ref, c_ref, out0_ref, out1_ref):
    straight = zh_ref[0] == 0
    extra = jnp.sum(got_ref[...].astype(jnp.float32), axis=0)
    halves = [got_ref[pl.ds(chip * 8, 8)].astype(jnp.float32) for chip in (c_ref[0], 1 - c_ref[0])]
    post = jnp.concatenate(halves, axis=0).reshape(128, 2 * LANES)
    post = jnp.where(iota((128, 2 * LANES), 1) % LANES < USED, post, 0.0)
    weights = jnp.transpose(post).astype(jnp.bfloat16)
    for h in range(2):
        cols = slice(h * HALF, (h + 1) * HALF)
        back = [
            jnp.dot(weights, joined(own_ref, other_ref, h, part), preferred_element_type=jnp.float32)
            for part in range(2)
        ]
        sums = [jnp.zeros((8, HALF), jnp.float32) for both in range(4)]
        for t in range(SHIFTS):
            cos, sin = cos_ref[t : t + 1, cols], sin_ref[t : t + 1, cols]
            for e in range(2):
                rows = slice(e * LANES + 8 * t, e * LANES + 8 * t + 8)
                back_re, back_im = back[0][rows], back[1][rows]
                sums[2 * e] += back_re * cos - back_im * sin
                sums[2 * e + 1] += back_im * cos + back_re * sin
        for part in range(2):
            low, high = sums[part].astype(jnp.bfloat16), sums[2 + part].astype(jnp.bfloat16)
            out0_ref[part, :, cols] = jnp.where(straight, low, high)
            out1_ref[part, :, cols] = jnp.where(straight, high, low)
    lane = iota((8, LANES), 1)
    masses = []
    for e in range(2):
        mine = (lane >= MASS) & (lane < MASS + 3)
        mass = jnp.sum(jnp.where(mine, extra[:, e * LANES : (e + 1) * LANES], 0.0), axis=1, keepdims=True)
        row = jnp.zeros((8, LANES), jnp.float32)
        for number, piece in enumerate(pieces_of(mass)):
            row = jnp.where(lane == number, piece, row)
        masses.append(row.astype(jnp.bfloat16))
    for part in range(2):
        out0_ref[part, :, PIXELS:] = jnp.where(straight, masses[0], masses[1])
        out1_ref[part, :, PIXELS:] = jnp.where(straight, masses[1], masses[0])


def final_kernel(first_ref, second_ref, out_ref):
    extra = first_ref[0, :, PIXELS:].astype(jnp.float32) + second_ref[0, :, PIXELS:].astype(jnp.float32)
    mass = jnp.sum(extra, axis=1, keepdims=True)
    for part in range(2):
        both = first_ref[part, :, :PIXELS].astype(jnp.float32) + second_ref[part, :, :PIXELS].astype(jnp.float32)
        out_ref[part] = both / (mass + 1.0)


def call(kernel, shapes, args, scratch=(), scalars=0, room=12, out_space=pltpu.VMEM):
    in_vmem = [pl.BlockSpec(memory_space=pltpu.VMEM)] * (len(args) - scalars)
    in_smem = [pl.BlockSpec(memory_space=pltpu.SMEM)] * scalars
    out = [jax.ShapeDtypeStruct(shape, dtype) for shape, dtype in shapes]
    return pl.pallas_call(
        kernel,
        out_shape=out,
        in_specs=in_vmem + in_smem,
        out_specs=[pl.BlockSpec(memory_space=out_space)] * len(out),
        scratch_shapes=list(scratch),
        compiler_params=pltpu.CompilerParams(vmem_limit_bytes=room << 20),
    )(*args)


def swap(operand, axes):
    return lax.all_to_all(operand, axes, 0, 0, tiled=True)


def local(images, references, precision, shifts, labels, log_prior):
    y, zh, c, zl, xh, xl = (lax.axis_index(name) for name in ALL)
    half = zh.astype(jnp.int32)[None]
    (sent,) = call(
        image_kernel,
        [((16, 2, 16, HALF + LANES), jnp.bfloat16)],
        (images, precision[None]),
        [pltpu.VMEM((2, 16, HALF + LANES), jnp.bfloat16), pltpu.SemaphoreType.DMA((16,))],
        room=60,
        out_space=pl.ANY,
    )
    units = swap(sent, SPACE).reshape(4, 2, 2, 2, 16, HALF + LANES)
    own = lax.dynamic_index_in_dim(units, c, 1, keepdims=False)
    other = lax.dynamic_index_in_dim(units, 1 - c, 1, keepdims=False)
    other = lax.ppermute(other, "c", SWAP)
    core = c.astype(jnp.int32)[None]
    (low,) = call(ref_kernel, [((2, 8, PIXELS + LANES), jnp.bfloat16)], (references, labels[None]))
    refs = [lax.ppermute(low, ALL, route) for route in routes(True)]
    cosine, sine = phases(shifts, zl * 2 + c)
    rotated = [
        call(
            rotate_kernel,
            [((2, LANES, PIXELS), jnp.bfloat16), ((2, LANES), jnp.float32)],
            (ref, cosine, sine),
            room=8,
        )
        for ref in refs
    ]
    (first, row0), (second, row1) = rotated
    (cross,) = call(
        cross_kernel,
        [((16, 8, 2 * LANES), jnp.float32)],
        (own, other, first, second, row0, row1, half, core),
        scalars=2,
        room=16,
    )
    scores, stats = call(
        score_kernel,
        [((8, 2 * LANES), jnp.float32), ((16, 8, LANES), jnp.float32)],
        (swap(cross, BLOCK), row0, row1, log_prior, half),
        scalars=2,
    )
    (post,) = call(post_kernel, [((16, 8, 2 * LANES), jnp.bfloat16)], (swap(stats, SPACE), scores), room=8)
    posts = swap(post, BLOCK)
    partial = call(
        back_kernel,
        [((2, 8, PIXELS + LANES), jnp.bfloat16)] * 2,
        (posts, own, other, cosine, sine, half, core),
        scalars=2,
    )
    first, second = [lax.ppermute(part, ALL, route) for part, route in zip(partial, routes(False), strict=True)]
    (new_refs,) = call(final_kernel, [((2, 8, PIXELS), jnp.float32)], (first, second))
    mine = lax.dynamic_slice_in_dim(posts, (c * 4 + y) * 2, 2, 0).reshape(16, 2 * LANES)
    shares = mine[:, CLASS : CLASS + 3 * CLASSES].astype(jnp.float32).reshape(16, 3, CLASSES)
    class_post = jnp.sum(shares, axis=1)
    return new_refs, class_post


def solution(mesh):
    whole = Mesh(mesh.devices.reshape(tuple(SIZES.values())), ALL)
    return jax.shard_map(
        local,
        mesh=whole,
        in_specs=(P(None, IMG, REF), P(None, REF, IMG), P(IMG), P(), P(REF), P()),
        out_specs=(P(None, REF, IMG), P(IMG, None)),
        check_vma=False,
    )
```
